512 devices in a mesh: grp: 16 (over y, core), tbl: 32 (over x, z).
Axes of the slice: x: 4, y: 8, z: 8, core: 2. Of those that a mesh axis runs over, the one named last changes fastest.
Arguments:
- dense_feats: bfloat16 [16384, 13], P(('grp', 'tbl')), may hold values from -6 to 6
- sparse_ids: int32 [26, 16384, 8], P(None, 'grp'), may hold values from 0 to 2047
- lengths: int32 [26, 16384], P(None, 'grp'), may hold values from 1 to 8
- table_map: int32 [26], replicated, may hold values from 0 to 63, as said below
- row_perm: int32 [16384], P(('grp', 'tbl')), may hold values from 0 to 16383, as said below
- tables: bfloat16 [64, 2048, 128], P('tbl'), may hold values from -2 to 2
- bottom_one: bfloat16 [13, 512], replicated, may hold values from -1.75 to 1.75
- bottom_two: bfloat16 [512, 256], replicated, may hold values from -0.25 to 0.25
- bottom_three: bfloat16 [256, 128], replicated, may hold values from -0.375 to 0.375
- top_one: bfloat16 [480, 4096], P(None, 'grp'), may hold values from -0.25 to 0.25
- top_two: bfloat16 [4096, 2048], P('grp'), may hold values from -0.09375 to 0.09375
- top_out: bfloat16 [2048], replicated, may hold values from -0.125 to 0.125
Outputs:
- probs: float32 [2, 16384], P(None, ('grp', 'tbl'))
The draws below stay inside these ranges and needn't reach their ends.
Inputs may be any that keep to these rules, and one draw needn't show every extreme that they name: `table_map`: distinct slots; no device of tbl holds more than 2 of the features' tables, and one holds exactly 2. A permutation of the rows; b and row_perm[b] have the same value of (b // 32) % 32.
All inputs are finite; a program needn't handle non-finite values.
Results may differ from the reference program's by a relative error of at most 0.0065.
Values may be sent and summed in bfloat16 or wider, within the bound.
No kernel may reach another device: no remote copies, remote signals or barrier semaphores. Data moves between devices by JAX's collectives and lax.ppermute only.
A program may use at most 64 MiB of HBM per device.

```python
import math
import jax
import jax.numpy as jnp
import numpy as np
from jax import lax

D = 128
F = 26
DENSE = 13
NPERM = 4
BAG = 8
VOCAB = 2048
BOT1 = 512
BOT2 = 256
H1 = 4096
H2 = 2048
ROWS = 32
CAP = 2
BATCH = 16384
ZW = 480
N_GRP = 16
N_TBL = 32


def draw_table_map(key, part):
    slot_total = CAP * N_TBL
    key_order, key_owner, key_feat = jax.random.split(key, 3)
    scores = jax.random.permutation(key_order, slot_total).astype(jnp.int32)
    busiest = jax.random.randint(key_owner, (), 0, N_TBL)
    slot_owner = jnp.arange(slot_total, dtype=jnp.int32) // CAP
    scores = jnp.where(slot_owner == busiest, scores - slot_total, scores)
    order = jnp.argsort(scores, stable=True)
    chosen = order[:F]
    return chosen[jax.random.permutation(key_feat, F)].astype(jnp.int32)


def draw_row_perm(key, part):
    span = N_GRP * ROWS

    def one_order(sub_key):
        return jax.random.permutation(sub_key, span).astype(jnp.int32)
    orders = jax.vmap(one_order)(jax.random.split(key, N_TBL))
    src_group = orders // ROWS
    src_pos = orders % ROWS
    owner_ids = jnp.arange(N_TBL, dtype=jnp.int32)[:, None]
    source = (src_group * N_TBL + owner_ids) * ROWS + src_pos
    return source.reshape(N_TBL, N_GRP, ROWS).transpose(1, 0, 2).reshape(-1).astype(jnp.int32)


def plant(entries, own_key, low, top_value):
    longest = entries.shape.index(max(entries.shape))
    spots = []
    for shift in (0, 1):
        where = [jax.random.randint(jax.random.fold_in(own_key, axis), (), 0, length) for axis, length in enumerate(entries.shape)]
        where[longest] = (where[longest] + shift) % entries.shape[longest]
        spots.append(tuple(where))
    return entries.at[spots[0]].set(low).at[spots[1]].set(top_value)


def level_of(key, extent, pieces, low, top_value):
    def one(dim, shards_of):
        steps = jax.random.uniform(jax.random.fold_in(jax.random.fold_in(key, 6), dim), (shards_of,), jnp.float32, low / len(pieces), top_value / len(pieces))
        return jnp.repeat(jnp.exp(steps), extent[dim] // shards_of).reshape((-1,) + (1,) * (len(extent) - dim - 1))

    factor_of = one(*pieces[0])
    for cut in pieces[1:]:
        factor_of = factor_of * one(*cut)
    return factor_of


def rank_table(count, slope):
    portions = [(1 << 20) // math.isqrt(grade ** slope) + 1 for grade in range(1, count + 1)]
    scale = 1 + sum(portions) // (1 << 30)
    return np.cumsum(np.array([max(1, weight // scale) for weight in portions]))


def ranked_ids(stream_key, shape, number_of, slope):
    grid = rank_table(number_of, slope)
    pick = jax.random.randint(jax.random.fold_in(stream_key, 1), shape, 0, int(grid[number_of - 1]))
    grade = jnp.searchsorted(jnp.asarray(grid, jnp.int32), pick, side="right")
    return jax.random.permutation(jax.random.fold_in(stream_key, 2), number_of)[grade].astype(jnp.int32)


def normal_values(rng, extent, scale, bound, shards=(), kind=jnp.bfloat16):
    result = scale * jax.random.normal(rng, extent, jnp.float32)
    if shards:
        result = result * level_of(rng, extent, shards, -0.22, 0.18)
    return jnp.clip(result, -bound, bound).astype(kind)


def setup_inputs(seed: int = 0) -> dict:
    keys = jax.random.split(jax.random.key(seed), 13)
    return {
        "dense_feats": normal_values(keys[0], (BATCH, DENSE), 1.0, 6.0, ((0, 512),)),
        "sparse_ids": plant(ranked_ids(keys[1], (F, BATCH, BAG), VOCAB, 2), jax.random.fold_in(keys[1], 3), 0, VOCAB - 1).astype(jnp.int32),
        "lengths": plant(jax.random.randint(keys[2], (F, BATCH), 1, BAG + 1), jax.random.fold_in(keys[2], 1), 1, BAG).astype(jnp.int32),
        "table_map": draw_table_map(jax.random.fold_in(keys[12], 71), 0),
        "row_perm": draw_row_perm(jax.random.fold_in(keys[12], 71), 0),
        "tables": normal_values(keys[5], (CAP * N_TBL, VOCAB, D), 0.15, 2.0, ((0, 32),)),
        "bottom_one": normal_values(keys[6], (DENSE, BOT1), DENSE ** -0.5, 1.75),
        "bottom_two": normal_values(keys[7], (BOT1, BOT2), BOT1 ** -0.5, 0.25),
        "bottom_three": normal_values(keys[8], (BOT2, D), BOT2 ** -0.5, 0.375),
        "top_one": normal_values(keys[9], (ZW, H1), ZW ** -0.5, 0.25, ((1, 16),)),
        "top_two": normal_values(keys[10], (H1, H2), H1 ** -0.5, 0.09375, ((0, 16),)),
        "top_out": normal_values(keys[11], (H2,), H2 ** -0.5, 0.125),
    }


def dense_layer(inputs, weights):
    return jnp.maximum(jnp.dot(inputs, weights, preferred_element_type=jnp.float32), 0.0).astype(jnp.bfloat16)


def make_codes(vectors, bottom_out):
    lower_idx, upper_idx = np.tril_indices(F + 1, -1)
    wide = vectors.astype(jnp.float32)
    gram = jnp.einsum("ibd,jbd->bij", wide, wide)
    pairs = gram[:, lower_idx, upper_idx]
    zero_col = jnp.zeros((bottom_out.shape[0], 1), jnp.float32)
    return jnp.concatenate([bottom_out.astype(jnp.float32), pairs, zero_col], axis=1).astype(jnp.bfloat16)


def reference(dense_feats, sparse_ids, lengths, table_map, row_perm, tables, bottom_one, bottom_two, bottom_three, top_one, top_two, top_out):
    bag_pos = jnp.arange(BAG, dtype=jnp.int32)

    def pool_feature(operands):
        feat_ids, feat_len, slot_idx = operands
        looked = tables[slot_idx][feat_ids].astype(jnp.float32)
        bag_mask = (bag_pos[None, :] < feat_len[:, None]).astype(jnp.float32)
        return jnp.einsum("bld,bl->bd", looked, bag_mask).astype(jnp.bfloat16)

    pooled = lax.map(pool_feature, (sparse_ids, lengths, table_map))
    bottom_out = dense_layer(dense_layer(dense_layer(dense_feats, bottom_one), bottom_two), bottom_three)
    shuffled = pooled[:NPERM][:, row_perm]
    vectors_base = jnp.concatenate([bottom_out[None], pooled], axis=0)
    vectors_perm = jnp.concatenate([bottom_out[None], shuffled, pooled[NPERM:]], axis=0)
    code_rows = jnp.concatenate([make_codes(vectors_base, bottom_out), make_codes(vectors_perm, bottom_out)], axis=0)
    hidden = dense_layer(code_rows, top_one)
    col_block = H1 // N_GRP
    summed = jnp.zeros((hidden.shape[0], H2), jnp.float32)
    for group_pos in range(N_GRP):
        part_sum = jnp.dot(hidden[:, group_pos * col_block:(group_pos + 1) * col_block], top_two[group_pos * col_block:(group_pos + 1) * col_block], preferred_element_type=jnp.float32)
        rounded = lax.optimization_barrier(part_sum.astype(jnp.bfloat16))
        summed = summed + rounded.astype(jnp.float32)
    logits = jnp.dot(jnp.maximum(summed, 0.0), top_out.astype(jnp.float32), precision=lax.Precision.HIGHEST)
    return jax.nn.sigmoid(logits).reshape(2, -1)
```

```python
import jax
import jax.numpy as jnp
import numpy as np
from jax import lax
from jax.experimental import pallas as pl
from jax.experimental.pallas import tpu as pltpu
from jax.sharding import PartitionSpec as P

NPERM = 4
LO = 256
ROWBLK = 16
TILE = 256


def dense_layer(inputs, weights):
    return jnp.maximum(jnp.dot(inputs, weights, preferred_element_type=jnp.float32), 0.0).astype(
        jnp.bfloat16
    )


def spread_bags(ids):
    sub = lax.broadcasted_iota(jnp.int32, ids.shape, 0)
    grp = lax.broadcasted_iota(jnp.int32, ids.shape, 1) // ROWBLK
    for step in (1, 2, 4):
        down = pltpu.roll(pltpu.roll(ids, 8 - step, 0), ROWBLK * step, 1)
        up = pltpu.roll(pltpu.roll(ids, step, 0), 128 - ROWBLK * step, 1)
        sub_bit = (sub & step) != 0
        grp_bit = (grp & step) != 0
        ids = jnp.where(sub_bit == grp_bit, ids, jnp.where(sub_bit, up, down))
    return ids


def pool_kernel(map_ref, owner_ref, ids_ref, len_ref, table_ref, out_ref, cnt_ref):
    vocab = table_ref.shape[1]
    hi_count = vocab // LO
    feat = find_feature(pl.program_id(0), map_ref, owner_ref)
    row_id = lax.broadcasted_iota(jnp.int32, (hi_count * ROWBLK, 128), 0)
    col_id = lax.broadcasted_iota(jnp.int32, (hi_count * ROWBLK, 128), 1)
    target = jnp.where(row_id % ROWBLK == col_id % ROWBLK, row_id // ROWBLK, -1)
    target = target.astype(jnp.float32).astype(jnp.bfloat16)
    lo_id = lax.broadcasted_iota(jnp.int32, (LO, 128), 0).astype(jnp.float32).astype(jnp.bfloat16)
    one = jnp.ones((), jnp.bfloat16)
    zero = jnp.zeros((), jnp.bfloat16)

    def tile(tile_idx, carry):
        for part in range(TILE // 128):
            start = pl.multiple_of(tile_idx * TILE + part * 128, 128)
            ids = ids_ref[0, :, pl.ds(start, 128)]
            lens = len_ref[:, pl.ds(start, 128)]
            feat_pos = lax.broadcasted_iota(jnp.int32, lens.shape, 0)
            lens = jnp.sum(jnp.where(feat_pos == feat, lens, 0), axis=0, keepdims=True)
            bag_pos = lax.broadcasted_iota(jnp.int32, ids.shape, 0)
            ids = spread_bags(jnp.where(bag_pos < lens, ids, vocab))
            high = (ids // LO).astype(jnp.float32)
            low = (ids % LO).astype(jnp.float32)
            for blk in range(8):
                high_row = jnp.broadcast_to(high[blk : blk + 1], target.shape).astype(jnp.bfloat16)
                low_row = jnp.broadcast_to(low[blk : blk + 1], lo_id.shape).astype(jnp.bfloat16)
                lhs = jnp.where(high_row == target, one, zero)
                rhs = jnp.where(low_row == lo_id, one, zero)
                counts = lax.dot_general(
                    lhs, rhs, (((1,), (1,)), ((), ())), preferred_element_type=jnp.float32
                ).astype(jnp.bfloat16)
                row = part * 128 + blk * ROWBLK
                for hi in range(hi_count):
                    cnt_ref[row : row + ROWBLK, hi * LO : (hi + 1) * LO] = counts[
                        hi * ROWBLK : (hi + 1) * ROWBLK
                    ]
        pooled = jnp.dot(cnt_ref[...], table_ref[0], preferred_element_type=jnp.float32)
        owners = TILE // out_ref.shape[2]
        out_ref[pl.ds(tile_idx * owners, owners), 0] = pooled.astype(jnp.bfloat16).reshape(
            owners, out_ref.shape[2], out_ref.shape[3]
        )
        return carry

    lax.fori_loop(0, ids_ref.shape[2] // TILE, tile, 0)


def find_feature(slot, map_ref, owner_ref):
    wanted = owner_ref[0] + slot
    feat = jnp.int32(0)
    for idx in range(map_ref.shape[0]):
        feat = jnp.where(map_ref[idx] == wanted, idx, feat)
    return feat


def pool_slots(table_map, first_slot, ids_t, lengths, tables, owners, row_count):
    slot_count, vocab, dim = tables.shape
    feats, bag, span = ids_t.shape
    return pl.pallas_call(
        pool_kernel,
        grid_spec=pltpu.PrefetchScalarGridSpec(
            num_scalar_prefetch=2,
            grid=(slot_count,),
            in_specs=[
                pl.BlockSpec(
                    (1, bag, span), lambda s, m, o: (find_feature(s, m, o), 0, 0)
                ),
                pl.BlockSpec((feats, span), lambda s, m, o: (0, 0)),
                pl.BlockSpec((1, vocab, dim), lambda s, m, o: (s, 0, 0)),
            ],
            out_specs=pl.BlockSpec(
                (owners, 1, row_count, dim), lambda s, m, o: (0, s, 0, 0)
            ),
            scratch_shapes=[pltpu.VMEM((TILE, vocab), jnp.bfloat16)],
        ),
        out_shape=jax.ShapeDtypeStruct((owners, slot_count, row_count, dim), jnp.bfloat16),
    )(table_map, first_slot, ids_t, lengths, tables)


def code_order(feats, dim, width):
    order = [0, *range(NPERM + 1, feats + 1), *range(1, NPERM + 1)]
    fixed = feats + 1 - NPERM

    def column(i, j):
        a, b = max(order[i], order[j]), min(order[i], order[j])
        return dim + a * (a - 1) // 2 + b

    cols = list(range(dim))
    cols += [column(i, j) for i in range(1, fixed) for j in range(i)]
    cols += [width - 1]
    cols += [-1] * (-len(cols) % 128)
    fixed_width = len(cols)
    cols += [column(i, j) for i in range(fixed, feats + 1) for j in range(i)]
    cols += [-1] * (-len(cols) % 128)
    return np.array(cols, np.int32), fixed_width


def fixed_codes(vectors, lead, fixed_width):
    gram = jnp.einsum("ird,jrd->rij", vectors, vectors, preferred_element_type=jnp.float32)
    pairs = [gram[:, level, :level] for level in range(1, vectors.shape[0])]
    out = jnp.concatenate([lead.astype(jnp.float32), *pairs], axis=1)
    return jnp.pad(out, ((0, 0), (0, fixed_width - out.shape[1]))).astype(jnp.bfloat16)


def moved_codes(moved, fixed, moved_width):
    every = jnp.concatenate([fixed, moved], axis=0)
    gram = jnp.einsum("ird,jrd->rij", moved, every, preferred_element_type=jnp.float32)
    pairs = [gram[:, i, : fixed.shape[0] + i] for i in range(moved.shape[0])]
    out = jnp.concatenate(pairs, axis=1)
    return jnp.pad(out, ((0, 0), (0, moved_width - out.shape[1]))).astype(jnp.bfloat16)


def top_kernel(core_ref, codes_ref, one_ref, own_ref, far_ref, out_w_ref, out_ref, acc_ref):
    step = pl.program_id(0)
    core = core_ref[0]
    width = codes_ref.shape[3]
    rows = codes_ref.shape[0] * codes_ref.shape[2]
    in_width = one_ref.shape[2]
    moved_width = width - in_width
    fixed_width = in_width - moved_width
    codes = jnp.concatenate([codes_ref[y, 0] for y in range(codes_ref.shape[0])], axis=0)
    fixed = codes[:, :fixed_width]
    moved = jnp.concatenate([codes[:, fixed_width:in_width], codes[:, in_width:]], axis=0)

    @pl.when(step == 0)
    def _():
        acc_ref[...] = jnp.zeros_like(acc_ref)

    total = acc_ref[...]
    for blk in range(own_ref.shape[0]):
        for side, second in ((core, own_ref), (1 - core, far_ref)):
            first = one_ref[blk, side]
            base = jnp.dot(fixed, first[:fixed_width], preferred_element_type=jnp.float32)
            delta = jnp.dot(moved, first[fixed_width:], preferred_element_type=jnp.float32)
            hidden = jnp.concatenate([base, base], axis=0) + delta
            hidden = jnp.maximum(hidden, 0.0).astype(jnp.bfloat16)
            total += jnp.dot(hidden, second[blk], preferred_element_type=jnp.float32)
    acc_ref[...] = total

    @pl.when(step == pl.num_programs(0) - 1)
    def _():
        scaled = jnp.maximum(total, 0.0) * out_w_ref[...]
        folded = scaled[:, :128]
        for lane in range(128, scaled.shape[1], 128):
            folded += scaled[:, lane : lane + 128]
        out_ref[...] = jnp.sum(folded.T, axis=0, keepdims=True)


def top_layers(core, codes, one_all, own, far, out_w):
    ys, cores, row_count, width = codes.shape
    in_width, blk_width = one_all.shape[2:]
    cols = own.shape[2]
    steps = 4 if ys % 4 == 0 else 1
    per = ys // steps
    return pl.pallas_call(
        top_kernel,
        grid_spec=pltpu.PrefetchScalarGridSpec(
            num_scalar_prefetch=1,
            grid=(steps,),
            in_specs=[
                pl.BlockSpec((ys, 1, row_count, width), lambda i, c: (0, c[0], 0, 0)),
                pl.BlockSpec((per, cores, in_width, blk_width), lambda i, c: (i, 0, 0, 0)),
                pl.BlockSpec((per, blk_width, cols), lambda i, c: (i, 0, 0)),
                pl.BlockSpec((per, blk_width, cols), lambda i, c: (i, 0, 0)),
                pl.BlockSpec((1, cols), lambda i, c: (0, 0)),
            ],
            out_specs=pl.BlockSpec((1, 2 * ys * row_count), lambda i, c: (0, 0)),
            scratch_shapes=[pltpu.VMEM((2 * ys * row_count, cols), jnp.float32)],
        ),
        out_shape=jax.ShapeDtypeStruct((1, 2 * ys * row_count), jnp.float32),
    )(core, codes, one_all, own, far, out_w)


def local(
    dense_feats,
    sparse_ids,
    lengths,
    table_map,
    row_perm,
    tables,
    bottom_one,
    bottom_two,
    bottom_three,
    top_one,
    top_two,
    top_out,
):
    groups = lax.axis_size("grp")
    owners = lax.axis_size("tbl")
    cores = 2
    ys = groups // cores
    grp_idx = lax.axis_index("grp")
    core = grp_idx % cores
    y_idx = grp_idx // cores
    same_core = [[cores * y + c for y in range(ys)] for c in range(cores)]
    swap_core = [(cores * y + c, cores * y + 1 - c) for y in range(ys) for c in range(cores)]
    slot_count = tables.shape[0]
    row_count = dense_feats.shape[0]
    feats = sparse_ids.shape[0]
    dim = tables.shape[2]

    cols, fixed_width = code_order(feats, dim, top_one.shape[0])
    in_width = cols.shape[0]
    moved_width = in_width - fixed_width
    pick_col = (jnp.asarray(cols)[:, None] == jnp.arange(top_one.shape[0])[None, :]).astype(
        jnp.bfloat16
    )
    one_local = jnp.dot(pick_col, top_one, preferred_element_type=jnp.float32).astype(jnp.bfloat16)
    one_all = lax.all_gather(one_local, "grp", axis=0, tiled=False)
    one_all = one_all.reshape(ys, cores, in_width, top_one.shape[1])

    out_cols = top_two.shape[1] // ys
    two_split = top_two.reshape(top_two.shape[0], ys, out_cols).transpose(1, 0, 2)
    own = lax.all_to_all(
        two_split, "grp", split_axis=0, concat_axis=0, tiled=True, axis_index_groups=same_core
    )
    far = lax.ppermute(own, "grp", swap_core)

    first_slot = (lax.axis_index("tbl") * slot_count).astype(jnp.int32).reshape(1)
    pooled = pool_slots(
        table_map, first_slot, sparse_ids.transpose(0, 2, 1), lengths, tables, owners, row_count
    )
    arrived = lax.all_to_all(pooled, "tbl", split_axis=0, concat_axis=0, tiled=True)
    arrived = arrived.reshape(owners * slot_count, row_count, dim)
    pick_slot = (
        table_map[:, None] == jnp.arange(owners * slot_count, dtype=jnp.int32)[None, :]
    ).astype(jnp.bfloat16)
    embedded = jnp.einsum(
        "fs,srd->frd", pick_slot, arrived, preferred_element_type=jnp.float32
    ).astype(jnp.bfloat16)

    bottom_out = dense_layer(
        dense_layer(dense_layer(dense_feats, bottom_one), bottom_two), bottom_three
    )
    gathered = lax.all_gather(embedded[:NPERM], "grp", axis=1, tiled=True)
    fixed = jnp.concatenate([bottom_out[None], embedded[NPERM:]], axis=0)
    code_fixed = fixed_codes(fixed, bottom_out, fixed_width)
    code_base = moved_codes(embedded[:NPERM], fixed, moved_width)
    source = row_perm // (owners * row_count) * row_count + row_perm % row_count
    pick_row = (source[:, None] == jnp.arange(gathered.shape[1], dtype=jnp.int32)[None, :]).astype(
        jnp.bfloat16
    )
    shuffled = jnp.einsum(
        "rs,psd->prd", pick_row, gathered, preferred_element_type=jnp.float32
    ).astype(jnp.bfloat16)
    code_perm = moved_codes(shuffled, fixed, moved_width)
    codes = jnp.concatenate([code_fixed, code_base, code_perm], axis=1)
    codes_all = lax.all_gather(codes, "grp", axis=0, tiled=False)
    codes_all = codes_all.reshape(ys, cores, row_count, codes.shape[1])

    out_w = lax.dynamic_slice(top_out, (y_idx * out_cols,), (out_cols,)).reshape(1, out_cols)
    out_w = out_w.astype(jnp.float32)
    part = top_layers(core.reshape(1), codes_all, one_all, own, far, out_w)
    part = part.reshape(2, ys, row_count).transpose(1, 0, 2)
    pieces = lax.all_to_all(
        part, "grp", split_axis=0, concat_axis=0, tiled=True, axis_index_groups=same_core
    )
    return jax.nn.sigmoid(jnp.sum(pieces, axis=0))


def solution(mesh):
    placed = (
        P(("grp", "tbl"), None),
        P(None, "grp", None),
        P(None, "grp"),
        P(),
        P(("grp", "tbl")),
        P("tbl", None, None),
        P(),
        P(),
        P(),
        P(None, "grp"),
        P("grp", None),
        P(),
    )
    return jax.shard_map(
        local, mesh=mesh, in_specs=placed, out_specs=P(None, ("grp", "tbl")), check_vma=False
    )
```

```python
import jax
import jax.numpy as jnp
import numpy as np
from jax import lax
from jax.experimental import pallas as pl
from jax.experimental.pallas import tpu as pltpu
from jax.sharding import PartitionSpec as P

NPERM = 4
LO = 256
ROWBLK = 16
TILE = 256


def dense_layer(inputs, weights):
    return jnp.maximum(jnp.dot(inputs, weights, preferred_element_type=jnp.float32), 0.0).astype(
        jnp.bfloat16
    )


def spread_bags(ids):
    sub = lax.broadcasted_iota(jnp.int32, ids.shape, 0)
    grp = lax.broadcasted_iota(jnp.int32, ids.shape, 1) // ROWBLK
    for step in (1, 2, 4):
        down = pltpu.roll(pltpu.roll(ids, 8 - step, 0), ROWBLK * step, 1)
        up = pltpu.roll(pltpu.roll(ids, step, 0), 128 - ROWBLK * step, 1)
        sub_bit = (sub & step) != 0
        grp_bit = (grp & step) != 0
        ids = jnp.where(sub_bit == grp_bit, ids, jnp.where(sub_bit, up, down))
    return ids


def pool_kernel(map_ref, owner_ref, ids_ref, len_ref, table_ref, out_ref, cnt_ref):
    vocab = table_ref.shape[1]
    hi_count = vocab // LO
    feat = find_feature(pl.program_id(0), map_ref, owner_ref)
    row_id = lax.broadcasted_iota(jnp.int32, (hi_count * ROWBLK, 128), 0)
    col_id = lax.broadcasted_iota(jnp.int32, (hi_count * ROWBLK, 128), 1)
    target = jnp.where(row_id % ROWBLK == col_id % ROWBLK, row_id // ROWBLK, -1)
    target = target.astype(jnp.float32).astype(jnp.bfloat16)
    lo_id = lax.broadcasted_iota(jnp.int32, (LO, 128), 0).astype(jnp.float32).astype(jnp.bfloat16)
    one = jnp.ones((), jnp.bfloat16)
    zero = jnp.zeros((), jnp.bfloat16)

    def tile(tile_idx, carry):
        for part in range(TILE // 128):
            start = pl.multiple_of(tile_idx * TILE + part * 128, 128)
            ids = ids_ref[0, :, pl.ds(start, 128)]
            lens = len_ref[:, pl.ds(start, 128)]
            feat_pos = lax.broadcasted_iota(jnp.int32, lens.shape, 0)
            lens = jnp.sum(jnp.where(feat_pos == feat, lens, 0), axis=0, keepdims=True)
            bag_pos = lax.broadcasted_iota(jnp.int32, ids.shape, 0)
            ids = spread_bags(jnp.where(bag_pos < lens, ids, vocab))
            high = (ids // LO).astype(jnp.float32)
            low = (ids % LO).astype(jnp.float32)
            for blk in range(8):
                high_row = jnp.broadcast_to(high[blk : blk + 1], target.shape).astype(jnp.bfloat16)
                low_row = jnp.broadcast_to(low[blk : blk + 1], lo_id.shape).astype(jnp.bfloat16)
                lhs = jnp.where(high_row == target, one, zero)
                rhs = jnp.where(low_row == lo_id, one, zero)
                counts = lax.dot_general(
                    lhs, rhs, (((1,), (1,)), ((), ())), preferred_element_type=jnp.float32
                ).astype(jnp.bfloat16)
                row = part * 128 + blk * ROWBLK
                for hi in range(hi_count):
                    cnt_ref[row : row + ROWBLK, hi * LO : (hi + 1) * LO] = counts[
                        hi * ROWBLK : (hi + 1) * ROWBLK
                    ]
        pooled = jnp.dot(cnt_ref[...], table_ref[0], preferred_element_type=jnp.float32)
        owners = TILE // out_ref.shape[2]
        out_ref[pl.ds(tile_idx * owners, owners), 0] = pooled.astype(jnp.bfloat16).reshape(
            owners, out_ref.shape[2], out_ref.shape[3]
        )
        return carry

    lax.fori_loop(0, ids_ref.shape[2] // TILE, tile, 0)


def find_feature(slot, map_ref, owner_ref):
    wanted = owner_ref[0] + slot
    feat = jnp.int32(0)
    for idx in range(map_ref.shape[0]):
        feat = jnp.where(map_ref[idx] == wanted, idx, feat)
    return feat


def pool_slots(table_map, first_slot, ids_t, lengths, tables, owners, row_count):
    slot_count, vocab, dim = tables.shape
    feats, bag, span = ids_t.shape
    return pl.pallas_call(
        pool_kernel,
        grid_spec=pltpu.PrefetchScalarGridSpec(
            num_scalar_prefetch=2,
            grid=(slot_count,),
            in_specs=[
                pl.BlockSpec(
                    (1, bag, span), lambda s, m, o: (find_feature(s, m, o), 0, 0)
                ),
                pl.BlockSpec((feats, span), lambda s, m, o: (0, 0)),
                pl.BlockSpec((1, vocab, dim), lambda s, m, o: (s, 0, 0)),
            ],
            out_specs=pl.BlockSpec(
                (owners, 1, row_count, dim), lambda s, m, o: (0, s, 0, 0)
            ),
            scratch_shapes=[pltpu.VMEM((TILE, vocab), jnp.bfloat16)],
        ),
        out_shape=jax.ShapeDtypeStruct((owners, slot_count, row_count, dim), jnp.bfloat16),
    )(table_map, first_slot, ids_t, lengths, tables)


def code_order(feats, dim, width):
    order = [0, *range(NPERM + 1, feats + 1), *range(1, NPERM + 1)]
    fixed = feats + 1 - NPERM

    def column(i, j):
        a, b = max(order[i], order[j]), min(order[i], order[j])
        return dim + a * (a - 1) // 2 + b

    cols = list(range(dim))
    cols += [column(i, j) for i in range(1, fixed) for j in range(i)]
    cols += [width - 1]
    cols += [-1] * (-len(cols) % 128)
    fixed_width = len(cols)
    cols += [column(i, j) for i in range(fixed, feats + 1) for j in range(i)]
    cols += [-1] * (-len(cols) % 128)
    return np.array(cols, np.int32), fixed_width


def fixed_codes(vectors, lead, fixed_width):
    gram = jnp.einsum("ird,jrd->rij", vectors, vectors, preferred_element_type=jnp.float32)
    pairs = [gram[:, level, :level] for level in range(1, vectors.shape[0])]
    out = jnp.concatenate([lead.astype(jnp.float32), *pairs], axis=1)
    return jnp.pad(out, ((0, 0), (0, fixed_width - out.shape[1]))).astype(jnp.bfloat16)


def moved_codes(moved, fixed, moved_width):
    every = jnp.concatenate([fixed, moved], axis=0)
    gram = jnp.einsum("ird,jrd->rij", moved, every, preferred_element_type=jnp.float32)
    pairs = [gram[:, i, : fixed.shape[0] + i] for i in range(moved.shape[0])]
    out = jnp.concatenate(pairs, axis=1)
    return jnp.pad(out, ((0, 0), (0, moved_width - out.shape[1]))).astype(jnp.bfloat16)


def top_kernel(pos_ref, codes_ref, one_ref, own_ref, far_ref, keep_ref, send_ref, acc_ref):
    step = pl.program_id(0)
    core = pos_ref[0]
    width = codes_ref.shape[3]
    in_width = one_ref.shape[2]
    moved_width = width - in_width
    fixed_width = in_width - moved_width
    codes = jnp.concatenate([codes_ref[y, 0] for y in range(codes_ref.shape[0])], axis=0)
    fixed = codes[:, :fixed_width]
    moved = jnp.concatenate([codes[:, fixed_width:in_width], codes[:, in_width:]], axis=0)

    @pl.when(step == 0)
    def _():
        acc_ref[...] = jnp.zeros_like(acc_ref)

    total = acc_ref[...]
    for side, second in ((core, own_ref), (1 - core, far_ref)):
        first = one_ref[0, side]
        base = jnp.dot(fixed, first[:fixed_width], preferred_element_type=jnp.float32)
        delta = jnp.dot(moved, first[fixed_width:], preferred_element_type=jnp.float32)
        hidden = jnp.concatenate([base, base], axis=0) + delta
        hidden = jnp.maximum(hidden, 0.0).astype(jnp.bfloat16)
        total += jnp.dot(hidden, second[0], preferred_element_type=jnp.float32)
    acc_ref[...] = total

    @pl.when(step == pl.num_programs(0) - 1)
    def _():
        half = total.shape[1] // 2
        low, high = total[:, :half], total[:, half:]
        is_low = pos_ref[2] == 0
        keep_ref[...] = jnp.where(is_low, low, high)
        send_ref[...] = jnp.where(is_low, high, low).astype(jnp.bfloat16)


def top_layers(pos, codes, one_all, own, far):
    ys, cores, row_count, width = codes.shape
    in_width, blk_width = one_all.shape[2:]
    quad, _, cols = own.shape
    rows = 2 * ys * row_count
    weights = pl.BlockSpec((1, blk_width, cols), lambda i, p: (i, 0, 0))
    result = pl.BlockSpec((rows, cols // 2), lambda i, p: (0, 0))
    return pl.pallas_call(
        top_kernel,
        grid_spec=pltpu.PrefetchScalarGridSpec(
            num_scalar_prefetch=1,
            grid=(quad,),
            in_specs=[
                pl.BlockSpec((ys, 1, row_count, width), lambda i, p: (0, p[0], 0, 0)),
                pl.BlockSpec(
                    (1, cores, in_width, blk_width), lambda i, p: ((p[1] + quad - i) % quad, 0, 0, 0)
                ),
                weights,
                weights,
            ],
            out_specs=[result, result],
            scratch_shapes=[pltpu.VMEM((rows, cols), jnp.float32)],
        ),
        out_shape=[
            jax.ShapeDtypeStruct((rows, cols // 2), jnp.float32),
            jax.ShapeDtypeStruct((rows, cols // 2), jnp.bfloat16),
        ],
    )(pos, codes, one_all, own, far)


def logit_kernel(keep_ref, came_ref, out_w_ref, out_ref):
    ys, variants, row_count = out_ref.shape
    total = keep_ref[...] + came_ref[...].astype(jnp.float32)
    scaled = jnp.maximum(total, 0.0) * out_w_ref[...]
    folded = scaled[:, :128]
    for lane in range(128, scaled.shape[1], 128):
        folded += scaled[:, lane : lane + 128]
    sums = jnp.sum(folded.T, axis=0, keepdims=True)
    for variant in range(variants):
        for y in range(ys):
            start = (variant * ys + y) * row_count
            out_ref[y, variant : variant + 1] = sums[:, start : start + row_count]


def local(
    dense_feats,
    sparse_ids,
    lengths,
    table_map,
    row_perm,
    tables,
    bottom_one,
    bottom_two,
    bottom_three,
    top_one,
    top_two,
    top_out,
):
    groups = lax.axis_size("grp")
    owners = lax.axis_size("tbl")
    cores = 2
    ys = groups // cores
    grp_idx = lax.axis_index("grp")
    core = grp_idx % cores
    y_idx = grp_idx // cores
    pairs = 2
    quad = ys // pairs
    same_core = [[cores * y + c for y in range(ys)] for c in range(cores)]
    swap_core = [(cores * y + c, cores * y + 1 - c) for y in range(ys) for c in range(cores)]
    swap_pair = [(cores * y + c, cores * (y ^ 1) + c) for y in range(ys) for c in range(cores)]
    same_parity = [
        [cores * y + c for y in range(h, ys, pairs) for c in range(cores)] for h in range(pairs)
    ]
    slot_count = tables.shape[0]
    row_count = dense_feats.shape[0]
    feats = sparse_ids.shape[0]
    dim = tables.shape[2]

    cols, fixed_width = code_order(feats, dim, top_one.shape[0])
    in_width = cols.shape[0]
    moved_width = in_width - fixed_width
    pick_col = (jnp.asarray(cols)[:, None] == jnp.arange(top_one.shape[0])[None, :]).astype(
        jnp.bfloat16
    )
    one_local = jnp.dot(pick_col, top_one, preferred_element_type=jnp.float32).astype(jnp.bfloat16)
    one_all = lax.all_gather(
        one_local, "grp", axis=0, tiled=False, axis_index_groups=same_parity
    )
    one_all = one_all.reshape(quad, cores, in_width, top_one.shape[1])

    blk_cols = top_two.shape[1] // quad
    blocks = []
    for hop in range(quad):
        start = (y_idx // pairs + hop) % quad * blk_cols
        piece = lax.dynamic_slice(top_two, (0, start), (top_two.shape[0], blk_cols))
        if hop:
            shift = [
                (cores * y + c, cores * ((y + pairs * hop) % ys) + c)
                for y in range(ys)
                for c in range(cores)
            ]
            piece = lax.ppermute(piece, "grp", shift)
        blocks.append(piece)
    first_slot = (lax.axis_index("tbl") * slot_count).astype(jnp.int32).reshape(1)
    pooled = pool_slots(
        table_map, first_slot, sparse_ids.transpose(0, 2, 1), lengths, tables, owners, row_count
    )
    arrived = lax.all_to_all(pooled, "tbl", split_axis=0, concat_axis=0, tiled=True)
    arrived = arrived.reshape(owners * slot_count, row_count, dim)
    pick_slot = (
        table_map[:, None] == jnp.arange(owners * slot_count, dtype=jnp.int32)[None, :]
    ).astype(jnp.bfloat16)
    embedded = jnp.einsum(
        "fs,srd->frd", pick_slot, arrived, preferred_element_type=jnp.float32
    ).astype(jnp.bfloat16)

    bottom_out = dense_layer(
        dense_layer(dense_layer(dense_feats, bottom_one), bottom_two), bottom_three
    )
    gathered = lax.all_gather(embedded[:NPERM], "grp", axis=1, tiled=True)
    gathered, *blocks = lax.optimization_barrier((gathered, *blocks))
    own = jnp.stack(blocks, axis=0)
    far = lax.ppermute(own, "grp", swap_core)
    fixed = jnp.concatenate([bottom_out[None], embedded[NPERM:]], axis=0)
    code_fixed = fixed_codes(fixed, bottom_out, fixed_width)
    code_base = moved_codes(embedded[:NPERM], fixed, moved_width)
    source = row_perm // (owners * row_count) * row_count + row_perm % row_count
    pick_row = (source[:, None] == jnp.arange(gathered.shape[1], dtype=jnp.int32)[None, :]).astype(
        jnp.bfloat16
    )
    shuffled = jnp.einsum(
        "rs,psd->prd", pick_row, gathered, preferred_element_type=jnp.float32
    ).astype(jnp.bfloat16)
    code_perm = moved_codes(shuffled, fixed, moved_width)
    codes = jnp.concatenate([code_fixed, code_base, code_perm], axis=1)
    codes_all = lax.all_gather(codes, "grp", axis=0, tiled=False)
    codes_all = codes_all.reshape(ys, cores, row_count, codes.shape[1])

    half = blk_cols // pairs
    parity = y_idx % pairs
    out_start = y_idx // pairs * blk_cols + parity * half
    out_w = lax.dynamic_slice(top_out, (out_start,), (half,)).reshape(1, half)
    out_w = out_w.astype(jnp.float32)
    pos = jnp.stack([core, y_idx // pairs, parity]).astype(jnp.int32)
    keep, send = top_layers(pos, codes_all, one_all, own, far)
    came = lax.ppermute(send, "grp", swap_pair)
    part = pl.pallas_call(
        logit_kernel, out_shape=jax.ShapeDtypeStruct((ys, 2, row_count), jnp.float32)
    )(keep, came, out_w)
    pieces = lax.all_to_all(
        part, "grp", split_axis=0, concat_axis=0, tiled=True, axis_index_groups=same_core
    )
    return jax.nn.sigmoid(jnp.sum(pieces, axis=0))


def solution(mesh):
    placed = (
        P(("grp", "tbl"), None),
        P(None, "grp", None),
        P(None, "grp"),
        P(),
        P(("grp", "tbl")),
        P("tbl", None, None),
        P(),
        P(),
        P(),
        P(None, "grp"),
        P("grp", None),
        P(),
    )
    return jax.shard_map(
        local, mesh=mesh, in_specs=placed, out_specs=P(None, ("grp", "tbl")), check_vma=False
    )
```

```python
import jax
import jax.numpy as jnp
import numpy as np
from jax import lax
from jax.experimental import pallas as pl
from jax.experimental.pallas import tpu as pltpu
from jax.sharding import PartitionSpec as P

NPERM = 4
LO = 256
ROWBLK = 16
TILE = 256


def dense_layer(inputs, weights):
    return jnp.maximum(jnp.dot(inputs, weights, preferred_element_type=jnp.float32), 0.0).astype(
        jnp.bfloat16
    )


def spread_bags(ids):
    sub = lax.broadcasted_iota(jnp.int32, ids.shape, 0)
    grp = lax.broadcasted_iota(jnp.int32, ids.shape, 1) // ROWBLK
    for step in (1, 2, 4):
        down = pltpu.roll(pltpu.roll(ids, 8 - step, 0), ROWBLK * step, 1)
        up = pltpu.roll(pltpu.roll(ids, step, 0), 128 - ROWBLK * step, 1)
        sub_bit = (sub & step) != 0
        grp_bit = (grp & step) != 0
        ids = jnp.where(sub_bit == grp_bit, ids, jnp.where(sub_bit, up, down))
    return ids


def pool_kernel(map_ref, owner_ref, ids_ref, len_ref, table_ref, out_ref, cnt_ref):
    vocab = table_ref.shape[1]
    hi_count = vocab // LO
    feat = find_feature(pl.program_id(0), map_ref, owner_ref)
    row_id = lax.broadcasted_iota(jnp.int32, (hi_count * ROWBLK, 128), 0)
    col_id = lax.broadcasted_iota(jnp.int32, (hi_count * ROWBLK, 128), 1)
    target = jnp.where(row_id % ROWBLK == col_id % ROWBLK, row_id // ROWBLK, -1)
    target = target.astype(jnp.float32).astype(jnp.bfloat16)
    lo_id = lax.broadcasted_iota(jnp.int32, (LO, 128), 0).astype(jnp.float32).astype(jnp.bfloat16)
    one = jnp.ones((), jnp.bfloat16)
    zero = jnp.zeros((), jnp.bfloat16)

    def tile(tile_idx, carry):
        for part in range(TILE // 128):
            start = pl.multiple_of(tile_idx * TILE + part * 128, 128)
            ids = ids_ref[0, :, pl.ds(start, 128)]
            lens = len_ref[:, pl.ds(start, 128)]
            feat_pos = lax.broadcasted_iota(jnp.int32, lens.shape, 0)
            lens = jnp.sum(jnp.where(feat_pos == feat, lens, 0), axis=0, keepdims=True)
            bag_pos = lax.broadcasted_iota(jnp.int32, ids.shape, 0)
            ids = spread_bags(jnp.where(bag_pos < lens, ids, vocab))
            high = (ids // LO).astype(jnp.float32)
            low = (ids % LO).astype(jnp.float32)
            for blk in range(8):
                high_row = jnp.broadcast_to(high[blk : blk + 1], target.shape).astype(jnp.bfloat16)
                low_row = jnp.broadcast_to(low[blk : blk + 1], lo_id.shape).astype(jnp.bfloat16)
                lhs = jnp.where(high_row == target, one, zero)
                rhs = jnp.where(low_row == lo_id, one, zero)
                counts = lax.dot_general(
                    lhs, rhs, (((1,), (1,)), ((), ())), preferred_element_type=jnp.float32
                ).astype(jnp.bfloat16)
                row = part * 128 + blk * ROWBLK
                for hi in range(hi_count):
                    cnt_ref[row : row + ROWBLK, hi * LO : (hi + 1) * LO] = counts[
                        hi * ROWBLK : (hi + 1) * ROWBLK
                    ]
        pooled = jnp.dot(cnt_ref[...], table_ref[0], preferred_element_type=jnp.float32)
        owners = TILE // out_ref.shape[2]
        out_ref[pl.ds(tile_idx * owners, owners), 0] = pooled.astype(jnp.bfloat16).reshape(
            owners, out_ref.shape[2], out_ref.shape[3]
        )
        return carry

    lax.fori_loop(0, ids_ref.shape[2] // TILE, tile, 0)


def find_feature(slot, map_ref, owner_ref):
    wanted = owner_ref[0] + slot
    feat = jnp.int32(0)
    for idx in range(map_ref.shape[0]):
        feat = jnp.where(map_ref[idx] == wanted, idx, feat)
    return feat


def pool_slots(table_map, first_slot, ids_t, lengths, tables, owners, row_count):
    slot_count, vocab, dim = tables.shape
    feats, bag, span = ids_t.shape
    return pl.pallas_call(
        pool_kernel,
        grid_spec=pltpu.PrefetchScalarGridSpec(
            num_scalar_prefetch=2,
            grid=(slot_count,),
            in_specs=[
                pl.BlockSpec(
                    (1, bag, span), lambda s, m, o: (find_feature(s, m, o), 0, 0)
                ),
                pl.BlockSpec((feats, span), lambda s, m, o: (0, 0)),
                pl.BlockSpec((1, vocab, dim), lambda s, m, o: (s, 0, 0)),
            ],
            out_specs=pl.BlockSpec(
                (owners, 1, row_count, dim), lambda s, m, o: (0, s, 0, 0)
            ),
            scratch_shapes=[pltpu.VMEM((TILE, vocab), jnp.bfloat16)],
        ),
        out_shape=jax.ShapeDtypeStruct((owners, slot_count, row_count, dim), jnp.bfloat16),
    )(table_map, first_slot, ids_t, lengths, tables)


def code_order(feats, dim, width):
    order = [0, *range(NPERM + 1, feats + 1), *range(1, NPERM + 1)]
    fixed = feats + 1 - NPERM

    def column(i, j):
        a, b = max(order[i], order[j]), min(order[i], order[j])
        return dim + a * (a - 1) // 2 + b

    cols = list(range(dim))
    cols += [column(i, j) for i in range(1, fixed) for j in range(i)]
    cols += [width - 1]
    cols += [-1] * (-len(cols) % 128)
    fixed_width = len(cols)
    cols += [column(i, j) for i in range(fixed, feats + 1) for j in range(i)]
    cols += [-1] * (-len(cols) % 128)
    return np.array(cols, np.int32), fixed_width


def fixed_codes(vectors, lead, fixed_width):
    gram = jnp.einsum("ird,jrd->rij", vectors, vectors, preferred_element_type=jnp.float32)
    pairs = [gram[:, level, :level] for level in range(1, vectors.shape[0])]
    out = jnp.concatenate([lead.astype(jnp.float32), *pairs], axis=1)
    return jnp.pad(out, ((0, 0), (0, fixed_width - out.shape[1]))).astype(jnp.bfloat16)


def moved_codes(moved, fixed, moved_width):
    every = jnp.concatenate([fixed, moved], axis=0)
    gram = jnp.einsum("ird,jrd->rij", moved, every, preferred_element_type=jnp.float32)
    pairs = [gram[:, i, : fixed.shape[0] + i] for i in range(moved.shape[0])]
    out = jnp.concatenate(pairs, axis=1)
    return jnp.pad(out, ((0, 0), (0, moved_width - out.shape[1]))).astype(jnp.bfloat16)


def top_kernel(codes_ref, weights_ref, out_w_ref, out_ref, acc_ref):
    step = pl.program_id(0)
    width = codes_ref.shape[2]
    blk_width = weights_ref.shape[2]
    in_width = weights_ref.shape[1] - blk_width
    moved_width = width - in_width
    fixed_width = in_width - moved_width
    codes = jnp.concatenate([codes_ref[z] for z in range(codes_ref.shape[0])], axis=0)
    fixed = codes[:, :fixed_width]
    moved = jnp.concatenate([codes[:, fixed_width:in_width], codes[:, in_width:]], axis=0)

    @pl.when(step == 0)
    def _():
        acc_ref[...] = jnp.zeros_like(acc_ref)

    total = acc_ref[...]
    for blk in range(weights_ref.shape[0]):
        base = jnp.dot(
            fixed, weights_ref[blk, :fixed_width], preferred_element_type=jnp.float32
        )
        delta = jnp.dot(
            moved, weights_ref[blk, fixed_width:in_width], preferred_element_type=jnp.float32
        )
        hidden = jnp.concatenate([base, base], axis=0) + delta
        hidden = jnp.maximum(hidden, 0.0).astype(jnp.bfloat16)
        total += jnp.dot(hidden, weights_ref[blk, in_width:], preferred_element_type=jnp.float32)
    acc_ref[...] = total

    @pl.when(step == pl.num_programs(0) - 1)
    def _():
        zs, variants, row_count = out_ref.shape
        scaled = jnp.maximum(total, 0.0) * out_w_ref[...]
        folded = scaled[:, :128]
        for lane in range(128, scaled.shape[1], 128):
            folded += scaled[:, lane : lane + 128]
        sums = jnp.sum(folded.T, axis=0, keepdims=True)
        for variant in range(variants):
            for z in range(zs):
                start = (variant * zs + z) * row_count
                out_ref[z, variant : variant + 1] = sums[:, start : start + row_count]


def top_layers(codes, weights, out_w):
    zs, row_count, width = codes.shape
    rows = zs * row_count
    groups, depth, blk_width = weights.shape
    steps = 4 if groups % 4 == 0 else 1
    return pl.pallas_call(
        top_kernel,
        grid=(steps,),
        in_specs=[
            pl.BlockSpec((zs, row_count, width), lambda i: (0, 0, 0)),
            pl.BlockSpec((groups // steps, depth, blk_width), lambda i: (i, 0, 0)),
            pl.BlockSpec((1, blk_width), lambda i: (0, 0)),
        ],
        out_specs=pl.BlockSpec((zs, 2, row_count), lambda i: (0, 0, 0)),
        scratch_shapes=[pltpu.VMEM((2 * rows, blk_width), jnp.float32)],
        out_shape=jax.ShapeDtypeStruct((zs, 2, row_count), jnp.float32),
    )(codes, weights, out_w)


def local(
    dense_feats,
    sparse_ids,
    lengths,
    table_map,
    row_perm,
    tables,
    bottom_one,
    bottom_two,
    bottom_three,
    top_one,
    top_two,
    top_out,
):
    owners = lax.axis_size("tbl")
    owner_idx = lax.axis_index("tbl")
    blk_cols = top_one.shape[1]
    zs = top_two.shape[1] // blk_cols
    z_idx = owner_idx % zs
    along_z = [[x * zs + z for z in range(zs)] for x in range(owners // zs)]
    slot_count = tables.shape[0]
    row_count = dense_feats.shape[0]
    feats = sparse_ids.shape[0]
    dim = tables.shape[2]

    cols, fixed_width = code_order(feats, dim, top_one.shape[0])
    in_width = cols.shape[0]
    moved_width = in_width - fixed_width
    pick_col = (jnp.asarray(cols)[:, None] == jnp.arange(top_one.shape[0])[None, :]).astype(
        jnp.bfloat16
    )
    one_local = jnp.dot(pick_col, top_one, preferred_element_type=jnp.float32).astype(jnp.bfloat16)
    two_local = lax.dynamic_slice(top_two, (0, z_idx * blk_cols), (top_two.shape[0], blk_cols))
    weights = lax.all_gather(
        jnp.concatenate([one_local, two_local], axis=0), "grp", axis=0, tiled=False
    )

    first_slot = (owner_idx * slot_count).astype(jnp.int32).reshape(1)
    pooled = pool_slots(
        table_map, first_slot, sparse_ids.transpose(0, 2, 1), lengths, tables, owners, row_count
    )
    arrived = lax.all_to_all(pooled, "tbl", split_axis=0, concat_axis=0, tiled=True)
    arrived = arrived.reshape(owners * slot_count, row_count, dim)
    pick_slot = (
        table_map[:, None] == jnp.arange(owners * slot_count, dtype=jnp.int32)[None, :]
    ).astype(jnp.bfloat16)
    embedded = jnp.einsum(
        "fs,srd->frd", pick_slot, arrived, preferred_element_type=jnp.float32
    ).astype(jnp.bfloat16)

    bottom_out = dense_layer(
        dense_layer(dense_layer(dense_feats, bottom_one), bottom_two), bottom_three
    )
    gathered = lax.all_gather(embedded[:NPERM], "grp", axis=1, tiled=True)
    fixed = jnp.concatenate([bottom_out[None], embedded[NPERM:]], axis=0)
    code_fixed = fixed_codes(fixed, bottom_out, fixed_width)
    code_base = moved_codes(embedded[:NPERM], fixed, moved_width)
    source = row_perm // (owners * row_count) * row_count + row_perm % row_count
    pick_row = (source[:, None] == jnp.arange(gathered.shape[1], dtype=jnp.int32)[None, :]).astype(
        jnp.bfloat16
    )
    shuffled = jnp.einsum(
        "rs,psd->prd", pick_row, gathered, preferred_element_type=jnp.float32
    ).astype(jnp.bfloat16)
    code_perm = moved_codes(shuffled, fixed, moved_width)
    codes = jnp.concatenate([code_fixed, code_base, code_perm], axis=1)
    codes_all = lax.all_gather(
        codes, "tbl", axis=0, tiled=False, axis_index_groups=along_z
    )
    out_w = lax.dynamic_slice(top_out, (z_idx * blk_cols,), (blk_cols,)).reshape(1, blk_cols)
    part = top_layers(codes_all, weights, out_w.astype(jnp.float32))
    pieces = lax.all_to_all(
        part, "tbl", split_axis=0, concat_axis=0, tiled=True, axis_index_groups=along_z
    )
    return jax.nn.sigmoid(jnp.sum(pieces, axis=0))


def solution(mesh):
    placed = (
        P(("grp", "tbl"), None),
        P(None, "grp", None),
        P(None, "grp"),
        P(),
        P(("grp", "tbl")),
        P("tbl", None, None),
        P(),
        P(),
        P(),
        P(None, "grp"),
        P("grp", None),
        P(),
    )
    return jax.shard_map(
        local, mesh=mesh, in_specs=placed, out_specs=P(None, ("grp", "tbl")), check_vma=False
    )
```

```python
import functools

import jax
import jax.numpy as jnp
import numpy as np
from jax import lax
from jax.experimental import pallas as pl
from jax.experimental.pallas import tpu as pltpu
from jax.sharding import PartitionSpec as P

NPERM = 4
LO = 256
ROWBLK = 16
TILE = 256
XS = 4


def dense_layer(inputs, weights):
    return jnp.maximum(jnp.dot(inputs, weights, preferred_element_type=jnp.float32), 0.0).astype(
        jnp.bfloat16
    )


def spread_bags(ids):
    sub = lax.broadcasted_iota(jnp.int32, ids.shape, 0)
    grp = lax.broadcasted_iota(jnp.int32, ids.shape, 1) // ROWBLK
    for step in (1, 2, 4):
        down = pltpu.roll(pltpu.roll(ids, 8 - step, 0), ROWBLK * step, 1)
        up = pltpu.roll(pltpu.roll(ids, step, 0), 128 - ROWBLK * step, 1)
        sub_bit = (sub & step) != 0
        grp_bit = (grp & step) != 0
        ids = jnp.where(sub_bit == grp_bit, ids, jnp.where(sub_bit, up, down))
    return ids


def pool_kernel(map_ref, owner_ref, ids_ref, len_ref, table_ref, out_ref, cnt_ref):
    vocab = table_ref.shape[1]
    hi_count = vocab // LO
    feat = find_feature(pl.program_id(0), map_ref, owner_ref)
    row_id = lax.broadcasted_iota(jnp.int32, (hi_count * ROWBLK, 128), 0)
    col_id = lax.broadcasted_iota(jnp.int32, (hi_count * ROWBLK, 128), 1)
    target = jnp.where(row_id % ROWBLK == col_id % ROWBLK, row_id // ROWBLK, -1)
    target = target.astype(jnp.float32).astype(jnp.bfloat16)
    lo_id = lax.broadcasted_iota(jnp.int32, (LO, 128), 0).astype(jnp.float32).astype(jnp.bfloat16)
    one = jnp.ones((), jnp.bfloat16)
    zero = jnp.zeros((), jnp.bfloat16)

    def tile(tile_idx, carry):
        for part in range(TILE // 128):
            start = pl.multiple_of(tile_idx * TILE + part * 128, 128)
            ids = ids_ref[0, :, pl.ds(start, 128)]
            lens = len_ref[:, pl.ds(start, 128)]
            feat_pos = lax.broadcasted_iota(jnp.int32, lens.shape, 0)
            lens = jnp.sum(jnp.where(feat_pos == feat, lens, 0), axis=0, keepdims=True)
            bag_pos = lax.broadcasted_iota(jnp.int32, ids.shape, 0)
            ids = spread_bags(jnp.where(bag_pos < lens, ids, vocab))
            high = (ids // LO).astype(jnp.float32)
            low = (ids % LO).astype(jnp.float32)
            for blk in range(8):
                high_row = jnp.broadcast_to(high[blk : blk + 1], target.shape).astype(jnp.bfloat16)
                low_row = jnp.broadcast_to(low[blk : blk + 1], lo_id.shape).astype(jnp.bfloat16)
                lhs = jnp.where(high_row == target, one, zero)
                rhs = jnp.where(low_row == lo_id, one, zero)
                counts = lax.dot_general(
                    lhs, rhs, (((1,), (1,)), ((), ())), preferred_element_type=jnp.float32
                ).astype(jnp.bfloat16)
                row = part * 128 + blk * ROWBLK
                for hi in range(hi_count):
                    cnt_ref[row : row + ROWBLK, hi * LO : (hi + 1) * LO] = counts[
                        hi * ROWBLK : (hi + 1) * ROWBLK
                    ]
        pooled = jnp.dot(cnt_ref[...], table_ref[0], preferred_element_type=jnp.float32)
        owners = TILE // out_ref.shape[2]
        out_ref[pl.ds(tile_idx * owners, owners), 0] = pooled.astype(jnp.bfloat16).reshape(
            owners, out_ref.shape[2], out_ref.shape[3]
        )
        return carry

    lax.fori_loop(0, ids_ref.shape[2] // TILE, tile, 0)


def find_feature(slot, map_ref, owner_ref):
    wanted = owner_ref[0] + slot
    feat = jnp.int32(0)
    for idx in range(map_ref.shape[0]):
        feat = jnp.where(map_ref[idx] == wanted, idx, feat)
    return feat


def pool_slots(table_map, first_slot, ids_t, lengths, tables, owners, row_count):
    slot_count, vocab, dim = tables.shape
    feats, bag, span = ids_t.shape
    return pl.pallas_call(
        pool_kernel,
        grid_spec=pltpu.PrefetchScalarGridSpec(
            num_scalar_prefetch=2,
            grid=(slot_count,),
            in_specs=[
                pl.BlockSpec(
                    (1, bag, span), lambda s, m, o: (find_feature(s, m, o), 0, 0)
                ),
                pl.BlockSpec((feats, span), lambda s, m, o: (0, 0)),
                pl.BlockSpec((1, vocab, dim), lambda s, m, o: (s, 0, 0)),
            ],
            out_specs=pl.BlockSpec(
                (owners, 1, row_count, dim), lambda s, m, o: (0, s, 0, 0)
            ),
            scratch_shapes=[pltpu.VMEM((TILE, vocab), jnp.bfloat16)],
        ),
        out_shape=jax.ShapeDtypeStruct((owners, slot_count, row_count, dim), jnp.bfloat16),
    )(table_map, first_slot, ids_t, lengths, tables)


def code_order(feats, dim, width):
    order = [0, *range(NPERM + 1, feats + 1), *range(1, NPERM + 1)]
    fixed = feats + 1 - NPERM

    def column(i, j):
        a, b = max(order[i], order[j]), min(order[i], order[j])
        return dim + a * (a - 1) // 2 + b

    cols = list(range(dim))
    cols += [column(i, j) for i in range(1, fixed) for j in range(i)]
    cols += [width - 1]
    cols += [-1] * (-len(cols) % 128)
    fixed_width = len(cols)
    cols += [column(i, j) for i in range(fixed, feats + 1) for j in range(i)]
    cols += [-1] * (-len(cols) % 128)
    return np.array(cols, np.int32), fixed_width


def fixed_codes(vectors, lead, fixed_width):
    gram = jnp.einsum("ird,jrd->rij", vectors, vectors, preferred_element_type=jnp.float32)
    pairs = [gram[:, level, :level] for level in range(1, vectors.shape[0])]
    out = jnp.concatenate([lead.astype(jnp.float32), *pairs], axis=1)
    return jnp.pad(out, ((0, 0), (0, fixed_width - out.shape[1]))).astype(jnp.bfloat16)


def moved_codes(moved, fixed, moved_width):
    every = jnp.concatenate([fixed, moved], axis=0)
    gram = jnp.einsum("ird,jrd->rij", moved, every, preferred_element_type=jnp.float32)
    pairs = [gram[:, i, : fixed.shape[0] + i] for i in range(moved.shape[0])]
    out = jnp.concatenate(pairs, axis=1)
    return jnp.pad(out, ((0, 0), (0, moved_width - out.shape[1]))).astype(jnp.bfloat16)


def top_kernel(in_width, codes_ref, weights_ref, out_w_ref, out_ref, acc_ref):
    step = pl.program_id(0)
    width = codes_ref.shape[2]
    blk_width = weights_ref.shape[2]
    moved_width = width - in_width
    fixed_width = in_width - moved_width
    codes = jnp.concatenate([codes_ref[z] for z in range(codes_ref.shape[0])], axis=0)
    fixed = codes[:, :fixed_width]
    moved = jnp.concatenate([codes[:, fixed_width:in_width], codes[:, in_width:]], axis=0)

    @pl.when(step == 0)
    def _():
        acc_ref[...] = jnp.zeros_like(acc_ref)

    total = acc_ref[...]
    for blk in range(weights_ref.shape[0]):
        base = jnp.dot(
            fixed, weights_ref[blk, :fixed_width], preferred_element_type=jnp.float32
        )
        delta = jnp.dot(
            moved, weights_ref[blk, fixed_width:in_width], preferred_element_type=jnp.float32
        )
        hidden = jnp.concatenate([base, base], axis=0) + delta
        hidden = jnp.maximum(hidden, 0.0).astype(jnp.bfloat16)
        total += jnp.concatenate(
            [
                jnp.dot(
                    hidden,
                    weights_ref[blk, start : start + blk_width],
                    preferred_element_type=jnp.float32,
                )
                for start in range(in_width, weights_ref.shape[1], blk_width)
            ],
            axis=1,
        )
    acc_ref[...] = total

    @pl.when(step == pl.num_programs(0) - 1)
    def _():
        zs, variants, row_count = out_ref.shape
        scaled = jnp.maximum(total, 0.0) * out_w_ref[...]
        folded = scaled[:, :128]
        for lane in range(128, scaled.shape[1], 128):
            folded += scaled[:, lane : lane + 128]
        sums = jnp.sum(folded.T, axis=0, keepdims=True)
        for variant in range(variants):
            for z in range(zs):
                start = (variant * zs + z) * row_count
                out_ref[z, variant : variant + 1] = sums[:, start : start + row_count]


def top_layers(codes, weights, out_w, in_width):
    zs, row_count, width = codes.shape
    rows = zs * row_count
    groups, depth, blk_width = weights.shape
    steps = 4 if groups % 4 == 0 else 1
    return pl.pallas_call(
        functools.partial(top_kernel, in_width),
        grid=(steps,),
        in_specs=[
            pl.BlockSpec((zs, row_count, width), lambda i: (0, 0, 0)),
            pl.BlockSpec((groups // steps, depth, blk_width), lambda i: (i, 0, 0)),
            pl.BlockSpec(out_w.shape, lambda i: (0, 0)),
        ],
        out_specs=pl.BlockSpec((zs, 2, row_count), lambda i: (0, 0, 0)),
        scratch_shapes=[pltpu.VMEM((2 * rows, out_w.shape[1]), jnp.float32)],
        out_shape=jax.ShapeDtypeStruct((zs, 2, row_count), jnp.float32),
    )(codes, weights, out_w)


def local(
    dense_feats,
    sparse_ids,
    lengths,
    table_map,
    row_perm,
    tables,
    bottom_one,
    bottom_two,
    bottom_three,
    top_one,
    top_two,
    top_out,
):
    owners = lax.axis_size("tbl")
    owner_idx = lax.axis_index("tbl")
    blk_cols = top_one.shape[1]
    xs = XS
    zs = owners // xs
    x_idx = owner_idx // zs
    along_x = [[x * zs + z for x in range(xs)] for z in range(zs)]
    out_cols = top_two.shape[1] // xs
    slot_count = tables.shape[0]
    row_count = dense_feats.shape[0]
    feats = sparse_ids.shape[0]
    dim = tables.shape[2]

    cols, fixed_width = code_order(feats, dim, top_one.shape[0])
    in_width = cols.shape[0]
    moved_width = in_width - fixed_width
    pick_col = (jnp.asarray(cols)[:, None] == jnp.arange(top_one.shape[0])[None, :]).astype(
        jnp.bfloat16
    )
    one_local = jnp.dot(pick_col, top_one, preferred_element_type=jnp.float32).astype(jnp.bfloat16)
    two_local = [
        lax.dynamic_slice(
            top_two, (0, x_idx * out_cols + start), (top_two.shape[0], blk_cols)
        )
        for start in range(0, out_cols, blk_cols)
    ]
    weights = lax.all_gather(
        jnp.concatenate([one_local, *two_local], axis=0), "grp", axis=0, tiled=False
    )

    first_slot = (owner_idx * slot_count).astype(jnp.int32).reshape(1)
    pooled = pool_slots(
        table_map, first_slot, sparse_ids.transpose(0, 2, 1), lengths, tables, owners, row_count
    )
    arrived = lax.all_to_all(pooled, "tbl", split_axis=0, concat_axis=0, tiled=True)
    arrived = arrived.reshape(owners * slot_count, row_count, dim)
    pick_slot = (
        table_map[:, None] == jnp.arange(owners * slot_count, dtype=jnp.int32)[None, :]
    ).astype(jnp.bfloat16)
    embedded = jnp.einsum(
        "fs,srd->frd", pick_slot, arrived, preferred_element_type=jnp.float32
    ).astype(jnp.bfloat16)

    bottom_out = dense_layer(
        dense_layer(dense_layer(dense_feats, bottom_one), bottom_two), bottom_three
    )
    gathered = lax.all_gather(embedded[:NPERM], "grp", axis=1, tiled=True)
    fixed = jnp.concatenate([bottom_out[None], embedded[NPERM:]], axis=0)
    code_fixed = fixed_codes(fixed, bottom_out, fixed_width)
    code_base = moved_codes(embedded[:NPERM], fixed, moved_width)
    source = row_perm // (owners * row_count) * row_count + row_perm % row_count
    pick_row = (source[:, None] == jnp.arange(gathered.shape[1], dtype=jnp.int32)[None, :]).astype(
        jnp.bfloat16
    )
    shuffled = jnp.einsum(
        "rs,psd->prd", pick_row, gathered, preferred_element_type=jnp.float32
    ).astype(jnp.bfloat16)
    code_perm = moved_codes(shuffled, fixed, moved_width)
    codes = jnp.concatenate([code_fixed, code_base, code_perm], axis=1)
    codes_all = lax.all_to_all(
        jnp.broadcast_to(codes[None], (xs, *codes.shape)),
        "tbl",
        split_axis=0,
        concat_axis=0,
        tiled=True,
        axis_index_groups=along_x,
    )
    out_w = lax.dynamic_slice(top_out, (x_idx * out_cols,), (out_cols,)).reshape(1, out_cols)
    part = top_layers(codes_all, weights, out_w.astype(jnp.float32), in_width)
    pieces = lax.all_to_all(
        part, "tbl", split_axis=0, concat_axis=0, tiled=True, axis_index_groups=along_x
    )
    return jax.nn.sigmoid(jnp.sum(pieces, axis=0))


def solution(mesh):
    placed = (
        P(("grp", "tbl"), None),
        P(None, "grp", None),
        P(None, "grp"),
        P(),
        P(("grp", "tbl")),
        P("tbl", None, None),
        P(),
        P(),
        P(),
        P(None, "grp"),
        P("grp", None),
        P(),
    )
    return jax.shard_map(
        local, mesh=mesh, in_specs=placed, out_specs=P(None, ("grp", "tbl")), check_vma=False
    )
```

```python
import functools

import jax
import jax.numpy as jnp
import numpy as np
from jax import lax
from jax.experimental import pallas as pl
from jax.experimental.pallas import tpu as pltpu
from jax.sharding import PartitionSpec as P

NPERM = 4
LO = 256
ROWBLK = 16
TILE = 512
XS = 4


def dense_layer(inputs, weights):
    return jnp.maximum(jnp.dot(inputs, weights, preferred_element_type=jnp.float32), 0.0).astype(
        jnp.bfloat16
    )


def spread_bags(ids):
    sub = lax.broadcasted_iota(jnp.int32, ids.shape, 0)
    grp = lax.broadcasted_iota(jnp.int32, ids.shape, 1) // ROWBLK
    for step in (1, 2, 4):
        down = pltpu.roll(pltpu.roll(ids, 8 - step, 0), ROWBLK * step, 1)
        up = pltpu.roll(pltpu.roll(ids, step, 0), 128 - ROWBLK * step, 1)
        sub_bit = (sub & step) != 0
        grp_bit = (grp & step) != 0
        ids = jnp.where(sub_bit == grp_bit, ids, jnp.where(sub_bit, up, down))
    return ids


def pool_kernel(map_ref, owner_ref, *refs):
    slot_count = len(refs) - 6
    ids_refs = refs[:slot_count]
    len_ref, table_ref, out_ref, cnt_ref, local_ref, sem = refs[slot_count:]
    vocab = table_ref.shape[1]
    hi_count = vocab // LO
    height = hi_count * ROWBLK
    span = len_ref.shape[1]
    fetch = pltpu.make_async_copy(table_ref, local_ref, sem)
    fetch.start()
    row_id = lax.broadcasted_iota(jnp.int32, (height, 128), 0)
    col_id = lax.broadcasted_iota(jnp.int32, (height, 128), 1)
    target = jnp.where(row_id % ROWBLK == col_id % ROWBLK, row_id // ROWBLK, -1)
    target = target.astype(jnp.float32).astype(jnp.bfloat16).reshape(-1, 16, 128)
    lo_id = lax.broadcasted_iota(jnp.int32, (LO, 128), 0)
    lo_id = lo_id.astype(jnp.float32).astype(jnp.bfloat16).reshape(-1, 16, 128)
    one = jnp.ones((), jnp.bfloat16)
    zero = jnp.zeros((), jnp.bfloat16)
    blank = jnp.zeros((height, 128), jnp.bfloat16)
    feat_pos = lax.broadcasted_iota(jnp.int32, len_ref.shape, 0)

    def one_hot(row, wanted):
        row = jnp.broadcast_to(row, (16, 128)).astype(jnp.bfloat16)
        return jnp.where(row[None] == wanted, one, zero).reshape(-1, 128)

    for slot in range(slot_count):
        feat = find_feature(slot, map_ref, owner_ref)
        lens = jnp.sum(jnp.where(feat_pos == feat, len_ref[...], 0), axis=0, keepdims=True)
        for start in range(0, span, 128):
            ids = ids_refs[slot][0, :, start : start + 128]
            bag_pos = lax.broadcasted_iota(jnp.int32, ids.shape, 0)
            ids = spread_bags(jnp.where(bag_pos < lens[:, start : start + 128], ids, vocab))
            high = (ids // LO).astype(jnp.float32)
            low = (ids % LO).astype(jnp.float32)
            for blk in range(0, 8, 2):
                lhs = [one_hot(high[i : i + 1], target) for i in (blk, blk + 1)]
                rhs = [one_hot(low[i : i + 1], lo_id) for i in (blk, blk + 1)]
                lhs = jnp.concatenate(
                    [
                        jnp.concatenate([lhs[0], blank], axis=1),
                        jnp.concatenate([blank, lhs[1]], axis=1),
                    ],
                    axis=0,
                )
                counts = lax.dot_general(
                    lhs,
                    jnp.concatenate(rhs, axis=1),
                    (((1,), (1,)), ((), ())),
                    preferred_element_type=jnp.float32,
                ).astype(jnp.bfloat16)
                for part in range(2 * hi_count):
                    row = start + (blk + part // hi_count) * ROWBLK
                    col = part % hi_count * LO
                    cnt_ref[slot, row : row + ROWBLK, col : col + LO] = counts[
                        part * ROWBLK : (part + 1) * ROWBLK
                    ]
        if slot == 0:
            fetch.wait()
        row_count = out_ref.shape[2]
        for start in range(0, span, TILE):
            pooled = jnp.dot(
                cnt_ref[slot, start : start + TILE],
                local_ref[slot],
                preferred_element_type=jnp.float32,
            ).astype(jnp.bfloat16)
            out_ref[start // row_count : (start + TILE) // row_count, slot] = pooled.reshape(
                TILE // row_count, row_count, out_ref.shape[3]
            )


def find_feature(slot, map_ref, owner_ref):
    wanted = owner_ref[0] + slot
    feat = jnp.int32(0)
    for idx in range(map_ref.shape[0]):
        feat = jnp.where(map_ref[idx] == wanted, idx, feat)
    return feat


def pool_slots(table_map, first_slot, ids_t, lengths, tables, owners, row_count):
    slot_count, vocab, dim = tables.shape
    feats, bag, span = ids_t.shape

    def ids_spec(slot):
        return pl.BlockSpec((1, bag, span), lambda i, m, o: (find_feature(slot, m, o), 0, 0))

    return pl.pallas_call(
        pool_kernel,
        grid_spec=pltpu.PrefetchScalarGridSpec(
            num_scalar_prefetch=2,
            grid=(1,),
            in_specs=[
                *[ids_spec(slot) for slot in range(slot_count)],
                pl.BlockSpec((feats, span), lambda i, m, o: (0, 0)),
                pl.BlockSpec(memory_space=pl.ANY),
            ],
            out_specs=pl.BlockSpec(
                (owners, slot_count, row_count, dim), lambda i, m, o: (0, 0, 0, 0)
            ),
            scratch_shapes=[
                pltpu.VMEM((slot_count, span, vocab), jnp.bfloat16),
                pltpu.VMEM(tables.shape, jnp.bfloat16),
                pltpu.SemaphoreType.DMA(()),
            ],
        ),
        out_shape=jax.ShapeDtypeStruct((owners, slot_count, row_count, dim), jnp.bfloat16),
    )(table_map, first_slot, *[ids_t] * slot_count, lengths, tables)


def pack_kernel(part_ref, cols_ref, one_ref, two_ref, out_ref, sems):
    blk_width = out_ref.shape[1]
    in_width = cols_ref.shape[1]
    count = (out_ref.shape[0] - in_width) // two_ref.shape[0]
    copies = []
    for blk in range(count):
        start = pl.multiple_of((part_ref[0] * count + blk) * blk_width, blk_width)
        copies.append(
            pltpu.make_async_copy(
                two_ref.at[:, pl.ds(start, blk_width)],
                out_ref.at[pl.ds(in_width + blk * two_ref.shape[0], two_ref.shape[0])],
                sems.at[blk],
            )
        )
        copies[-1].start()
    row = lax.broadcasted_iota(jnp.int32, (one_ref.shape[0], in_width), 0)
    pick = jnp.where(row == cols_ref[...], 1.0, 0.0).astype(jnp.bfloat16)
    out_ref[:in_width] = lax.dot_general(
        pick, one_ref[...], (((0,), (0,)), ((), ())), preferred_element_type=jnp.float32
    ).astype(jnp.bfloat16)
    for copy in copies:
        copy.wait()


def pack_weights(part, cols, top_one, top_two, out_cols):
    blk_width = top_one.shape[1]
    count = out_cols // blk_width
    whole = pl.BlockSpec(memory_space=pltpu.VMEM)
    rows = cols.shape[0] + count * top_two.shape[0]
    return pl.pallas_call(
        pack_kernel,
        in_specs=[
            pl.BlockSpec(memory_space=pltpu.SMEM),
            whole,
            whole,
            pl.BlockSpec(memory_space=pl.ANY),
        ],
        out_specs=whole,
        scratch_shapes=[pltpu.SemaphoreType.DMA((count,))],
        out_shape=jax.ShapeDtypeStruct((rows, blk_width), jnp.bfloat16),
    )(part.reshape(1), jnp.asarray(cols)[None], top_one, top_two)


def code_order(feats, dim, width):
    order = [0, *range(NPERM + 1, feats + 1), *range(1, NPERM + 1)]
    fixed = feats + 1 - NPERM

    def column(i, j):
        a, b = max(order[i], order[j]), min(order[i], order[j])
        return dim + a * (a - 1) // 2 + b

    cols = list(range(dim))
    cols += [column(i, j) for i in range(1, fixed) for j in range(i)]
    cols += [width - 1]
    cols += [-1] * (-len(cols) % 128)
    fixed_width = len(cols)
    cols += [column(i, j) for i in range(fixed, feats + 1) for j in range(i)]
    cols += [-1] * (-len(cols) % 128)
    return np.array(cols, np.int32), fixed_width


def fixed_codes(vectors, lead, fixed_width):
    gram = jnp.einsum("ird,jrd->rij", vectors, vectors, preferred_element_type=jnp.float32)
    pairs = [gram[:, level, :level] for level in range(1, vectors.shape[0])]
    out = jnp.concatenate([lead.astype(jnp.float32), *pairs], axis=1)
    return jnp.pad(out, ((0, 0), (0, fixed_width - out.shape[1]))).astype(jnp.bfloat16)


def moved_codes(moved, fixed, moved_width):
    every = jnp.concatenate([fixed, moved], axis=0)
    gram = jnp.einsum("ird,jrd->rij", moved, every, preferred_element_type=jnp.float32)
    pairs = [gram[:, i, : fixed.shape[0] + i] for i in range(moved.shape[0])]
    out = jnp.concatenate(pairs, axis=1)
    return jnp.pad(out, ((0, 0), (0, moved_width - out.shape[1]))).astype(jnp.bfloat16)


def top_kernel(in_width, codes_ref, weights_ref, out_w_ref, out_ref, acc_ref, codes_all_ref):
    step = pl.program_id(0)
    blk_width = weights_ref.shape[2]
    fixed_width = 2 * in_width - codes_ref.shape[2]

    @pl.when(step == 0)
    def _():
        codes = jnp.concatenate([codes_ref[x] for x in range(codes_ref.shape[0])], axis=0)
        rows = codes.shape[0]
        codes_all_ref[:rows] = codes[:, :in_width]
        codes_all_ref[rows:, :fixed_width] = codes[:, :fixed_width]
        codes_all_ref[rows:, fixed_width:] = codes[:, in_width:]
        acc_ref[...] = jnp.zeros_like(acc_ref)

    codes = codes_all_ref[...]
    hidden = []
    for blk in range(weights_ref.shape[0]):
        pre = jnp.dot(codes, weights_ref[blk, :in_width], preferred_element_type=jnp.float32)
        hidden.append(jnp.maximum(pre, 0.0).astype(jnp.bfloat16))
    for col in range(0, acc_ref.shape[1], blk_width):
        total = acc_ref[:, col : col + blk_width]
        row = in_width + col // blk_width * blk_width
        for blk in range(weights_ref.shape[0]):
            total += jnp.dot(
                hidden[blk],
                weights_ref[blk, row : row + blk_width],
                preferred_element_type=jnp.float32,
            )
        acc_ref[:, col : col + blk_width] = total

    @pl.when(step == pl.num_programs(0) - 1)
    def _():
        xs, variants, row_count = out_ref.shape
        scaled = jnp.maximum(acc_ref[...], 0.0) * out_w_ref[...]
        folded = scaled[:, :128]
        for lane in range(128, scaled.shape[1], 128):
            folded += scaled[:, lane : lane + 128]
        sums = jnp.sum(folded.T, axis=0, keepdims=True)
        for variant in range(variants):
            for x in range(xs):
                start = (variant * xs + x) * row_count
                out_ref[x, variant : variant + 1] = sums[:, start : start + row_count]


def top_layers(codes, weights, out_w, in_width):
    xs, row_count, _ = codes.shape
    groups, depth, blk_width = weights.shape
    steps = 2
    rows = 2 * xs * row_count
    return pl.pallas_call(
        functools.partial(top_kernel, in_width),
        grid=(steps,),
        in_specs=[
            pl.BlockSpec(memory_space=pltpu.VMEM),
            pl.BlockSpec((groups // steps, depth, blk_width), lambda i: (i, 0, 0)),
            pl.BlockSpec(memory_space=pltpu.VMEM),
        ],
        out_specs=pl.BlockSpec((xs, 2, row_count), lambda i: (0, 0, 0)),
        scratch_shapes=[
            pltpu.VMEM((rows, out_w.shape[1]), jnp.float32),
            pltpu.VMEM((rows, in_width), jnp.bfloat16),
        ],
        out_shape=jax.ShapeDtypeStruct((xs, 2, row_count), jnp.float32),
    )(codes, weights, out_w)


def local(
    dense_feats,
    sparse_ids,
    lengths,
    table_map,
    row_perm,
    tables,
    bottom_one,
    bottom_two,
    bottom_three,
    top_one,
    top_two,
    top_out,
):
    owners = lax.axis_size("tbl")
    owner_idx = lax.axis_index("tbl")
    xs = XS
    zs = owners // xs
    x_idx = owner_idx // zs
    along_x = [[x * zs + z for x in range(xs)] for z in range(zs)]
    out_cols = top_two.shape[1] // xs
    slot_count = tables.shape[0]
    row_count = dense_feats.shape[0]
    feats = sparse_ids.shape[0]
    dim = tables.shape[2]

    cols, fixed_width = code_order(feats, dim, top_one.shape[0])
    in_width = cols.shape[0]
    moved_width = in_width - fixed_width
    packed = pack_weights(x_idx.astype(jnp.int32), cols, top_one, top_two, out_cols)
    weights = lax.all_gather(packed, "grp", axis=0, tiled=False)

    first_slot = (owner_idx * slot_count).astype(jnp.int32).reshape(1)
    pooled = pool_slots(
        table_map, first_slot, sparse_ids.transpose(0, 2, 1), lengths, tables, owners, row_count
    )
    arrived = lax.all_to_all(pooled, "tbl", split_axis=0, concat_axis=0, tiled=True)
    arrived = arrived.reshape(owners * slot_count, row_count, dim)
    pick_slot = (
        table_map[:, None] == jnp.arange(owners * slot_count, dtype=jnp.int32)[None, :]
    ).astype(jnp.bfloat16)
    embedded = jnp.einsum(
        "fs,srd->frd", pick_slot, arrived, preferred_element_type=jnp.float32
    ).astype(jnp.bfloat16)

    bottom_out = dense_layer(
        dense_layer(dense_layer(dense_feats, bottom_one), bottom_two), bottom_three
    )
    gathered = lax.all_gather(embedded[:NPERM], "grp", axis=1, tiled=True)
    fixed = jnp.concatenate([bottom_out[None], embedded[NPERM:]], axis=0)
    code_fixed = fixed_codes(fixed, bottom_out, fixed_width)
    code_base = moved_codes(embedded[:NPERM], fixed, moved_width)
    source = row_perm // (owners * row_count) * row_count + row_perm % row_count
    pick_row = (source[:, None] == jnp.arange(gathered.shape[1], dtype=jnp.int32)[None, :]).astype(
        jnp.bfloat16
    )
    shuffled = jnp.einsum(
        "rs,psd->prd", pick_row, gathered, preferred_element_type=jnp.float32
    ).astype(jnp.bfloat16)
    code_perm = moved_codes(shuffled, fixed, moved_width)
    codes = jnp.concatenate([code_fixed, code_base, code_perm], axis=1)
    codes_all = lax.all_to_all(
        jnp.broadcast_to(codes[None], (xs, *codes.shape)),
        "tbl",
        split_axis=0,
        concat_axis=0,
        tiled=True,
        axis_index_groups=along_x,
    )
    out_w = lax.dynamic_slice(top_out, (x_idx * out_cols,), (out_cols,)).reshape(1, out_cols)
    part = top_layers(codes_all, weights, out_w.astype(jnp.float32), in_width)
    pieces = lax.all_to_all(
        part, "tbl", split_axis=0, concat_axis=0, tiled=True, axis_index_groups=along_x
    )
    return jax.nn.sigmoid(jnp.sum(pieces, axis=0))


def solution(mesh):
    placed = (
        P(("grp", "tbl"), None),
        P(None, "grp", None),
        P(None, "grp"),
        P(),
        P(("grp", "tbl")),
        P("tbl", None, None),
        P(),
        P(),
        P(),
        P(None, "grp"),
        P("grp", None),
        P(),
    )
    return jax.shard_map(
        local, mesh=mesh, in_specs=placed, out_specs=P(None, ("grp", "tbl")), check_vma=False
    )
```

```python
import functools

import jax
import jax.numpy as jnp
import numpy as np
from jax import lax
from jax.experimental import pallas as pl
from jax.experimental.pallas import tpu as pltpu
from jax.sharding import PartitionSpec as P

NPERM = 4
LO = 256
ROWBLK = 16
TILE = 512
XS = 4


def dense_layer(inputs, weights):
    return jnp.maximum(jnp.dot(inputs, weights, preferred_element_type=jnp.float32), 0.0).astype(
        jnp.bfloat16
    )


def spread_bags(ids):
    sub = lax.broadcasted_iota(jnp.int32, ids.shape, 0)
    grp = lax.broadcasted_iota(jnp.int32, ids.shape, 1) // ROWBLK
    for step in (1, 2, 4):
        down = pltpu.roll(pltpu.roll(ids, 8 - step, 0), ROWBLK * step, 1)
        up = pltpu.roll(pltpu.roll(ids, step, 0), 128 - ROWBLK * step, 1)
        sub_bit = (sub & step) != 0
        grp_bit = (grp & step) != 0
        ids = jnp.where(sub_bit == grp_bit, ids, jnp.where(sub_bit, up, down))
    return ids


def pool_kernel(map_ref, owner_ref, part_ref, *refs):
    slot_count = len(refs) - 13
    ids_refs = refs[:slot_count]
    len_ref, cols_ref, table_ref, one_ref, two_ref, out_ref, packed_ref = refs[slot_count:-6]
    cnt_ref, local_ref, first_ref, pack_ref, sem, sems = refs[-6:]
    vocab = table_ref.shape[1]
    hi_count = vocab // LO
    height = hi_count * ROWBLK
    span = len_ref.shape[1]
    fetch = pltpu.make_async_copy(table_ref, local_ref, sem)
    fetch.start()
    in_width = cols_ref.shape[1]
    depth, blk_width = two_ref.shape[0], one_ref.shape[1]
    count = (pack_ref.shape[0] - in_width) // depth
    loads = [pltpu.make_async_copy(one_ref, first_ref, sems.at[0])]
    for blk in range(count):
        start = pl.multiple_of((part_ref[0] * count + blk) * blk_width, blk_width)
        loads.append(
            pltpu.make_async_copy(
                two_ref.at[:, pl.ds(start, blk_width)],
                pack_ref.at[pl.ds(in_width + blk * depth, depth)],
                sems.at[1 + blk],
            )
        )
    for load in loads:
        load.start()
    send = pltpu.make_async_copy(pack_ref, packed_ref, sems.at[1 + count])
    row_id = lax.broadcasted_iota(jnp.int32, (height, 128), 0)
    col_id = lax.broadcasted_iota(jnp.int32, (height, 128), 1)
    target = jnp.where(row_id % ROWBLK == col_id % ROWBLK, row_id // ROWBLK, -1)
    target = target.astype(jnp.float32).astype(jnp.bfloat16).reshape(-1, 16, 128)
    lo_id = lax.broadcasted_iota(jnp.int32, (LO, 128), 0)
    lo_id = lo_id.astype(jnp.float32).astype(jnp.bfloat16).reshape(-1, 16, 128)
    one = jnp.ones((), jnp.bfloat16)
    zero = jnp.zeros((), jnp.bfloat16)
    blank = jnp.zeros((height, 128), jnp.bfloat16)
    feat_pos = lax.broadcasted_iota(jnp.int32, len_ref.shape, 0)

    def one_hot(row, wanted):
        row = jnp.broadcast_to(row, (16, 128)).astype(jnp.bfloat16)
        return jnp.where(row[None] == wanted, one, zero).reshape(-1, 128)

    for slot in range(slot_count):
        feat = find_feature(slot, map_ref, owner_ref)
        lens = jnp.sum(jnp.where(feat_pos == feat, len_ref[...], 0), axis=0, keepdims=True)
        for start in range(0, span, 128):
            ids = ids_refs[slot][0, :, start : start + 128]
            bag_pos = lax.broadcasted_iota(jnp.int32, ids.shape, 0)
            ids = spread_bags(jnp.where(bag_pos < lens[:, start : start + 128], ids, vocab))
            high = (ids // LO).astype(jnp.float32)
            low = (ids % LO).astype(jnp.float32)
            for blk in range(0, 8, 2):
                lhs = [one_hot(high[i : i + 1], target) for i in (blk, blk + 1)]
                rhs = [one_hot(low[i : i + 1], lo_id) for i in (blk, blk + 1)]
                lhs = jnp.concatenate(
                    [
                        jnp.concatenate([lhs[0], blank], axis=1),
                        jnp.concatenate([blank, lhs[1]], axis=1),
                    ],
                    axis=0,
                )
                counts = lax.dot_general(
                    lhs,
                    jnp.concatenate(rhs, axis=1),
                    (((1,), (1,)), ((), ())),
                    preferred_element_type=jnp.float32,
                ).astype(jnp.bfloat16)
                for part in range(2 * hi_count):
                    row = start + (blk + part // hi_count) * ROWBLK
                    col = part % hi_count * LO
                    cnt_ref[slot, row : row + ROWBLK, col : col + LO] = counts[
                        part * ROWBLK : (part + 1) * ROWBLK
                    ]
        if slot == 0:
            for load in loads:
                load.wait()
            row = lax.broadcasted_iota(jnp.int32, (first_ref.shape[0], in_width), 0)
            pick = jnp.where(row == cols_ref[...], 1.0, 0.0).astype(jnp.bfloat16)
            pack_ref[:in_width] = lax.dot_general(
                pick, first_ref[...], (((0,), (0,)), ((), ())), preferred_element_type=jnp.float32
            ).astype(jnp.bfloat16)
            send.start()
            fetch.wait()
        row_count = out_ref.shape[2]
        for start in range(0, span, TILE):
            pooled = jnp.dot(
                cnt_ref[slot, start : start + TILE],
                local_ref[slot],
                preferred_element_type=jnp.float32,
            ).astype(jnp.bfloat16)
            out_ref[start // row_count : (start + TILE) // row_count, slot] = pooled.reshape(
                TILE // row_count, row_count, out_ref.shape[3]
            )
    send.wait()


def find_feature(slot, map_ref, owner_ref):
    wanted = owner_ref[0] + slot
    feat = jnp.int32(0)
    for idx in range(map_ref.shape[0]):
        feat = jnp.where(map_ref[idx] == wanted, idx, feat)
    return feat


def pool_slots(
    table_map, first_slot, part, ids_t, lengths, tables, cols, top_one, top_two, dims
):
    owners, row_count, out_cols = dims
    slot_count, vocab, dim = tables.shape
    feats, bag, span = ids_t.shape
    blk_width = top_one.shape[1]
    count = out_cols // blk_width
    packed = (cols.shape[0] + count * top_two.shape[0], blk_width)
    pooled = (owners, slot_count, row_count, dim)
    away = pl.BlockSpec(memory_space=pl.ANY)

    def ids_spec(slot):
        return pl.BlockSpec((1, bag, span), lambda i, m, o, p: (find_feature(slot, m, o), 0, 0))

    return pl.pallas_call(
        pool_kernel,
        grid_spec=pltpu.PrefetchScalarGridSpec(
            num_scalar_prefetch=3,
            grid=(1,),
            in_specs=[
                *[ids_spec(slot) for slot in range(slot_count)],
                pl.BlockSpec((feats, span), lambda i, m, o, p: (0, 0)),
                pl.BlockSpec((1, cols.shape[0]), lambda i, m, o, p: (0, 0)),
                away,
                away,
                away,
            ],
            out_specs=[pl.BlockSpec(pooled, lambda i, m, o, p: (0, 0, 0, 0)), away],
            scratch_shapes=[
                pltpu.VMEM((slot_count, span, vocab), jnp.bfloat16),
                pltpu.VMEM(tables.shape, jnp.bfloat16),
                pltpu.VMEM(top_one.shape, jnp.bfloat16),
                pltpu.VMEM(packed, jnp.bfloat16),
                pltpu.SemaphoreType.DMA(()),
                pltpu.SemaphoreType.DMA((count + 2,)),
            ],
        ),
        out_shape=[
            jax.ShapeDtypeStruct(pooled, jnp.bfloat16),
            jax.ShapeDtypeStruct(packed, jnp.bfloat16),
        ],
    )(
        table_map,
        first_slot,
        part,
        *[ids_t] * slot_count,
        lengths,
        jnp.asarray(cols)[None],
        tables,
        top_one,
        top_two,
    )


def code_order(feats, dim, width):
    order = [0, *range(NPERM + 1, feats + 1), *range(1, NPERM + 1)]
    fixed = feats + 1 - NPERM

    def column(i, j):
        a, b = max(order[i], order[j]), min(order[i], order[j])
        return dim + a * (a - 1) // 2 + b

    cols = list(range(dim))
    cols += [column(i, j) for i in range(1, fixed) for j in range(i)]
    cols += [width - 1]
    cols += [-1] * (-len(cols) % 128)
    fixed_width = len(cols)
    cols += [column(i, j) for i in range(fixed, feats + 1) for j in range(i)]
    cols += [-1] * (-len(cols) % 128)
    return np.array(cols, np.int32), fixed_width


def fixed_codes(vectors, lead, fixed_width):
    gram = jnp.einsum("ird,jrd->rij", vectors, vectors, preferred_element_type=jnp.float32)
    pairs = [gram[:, level, :level] for level in range(1, vectors.shape[0])]
    out = jnp.concatenate([lead.astype(jnp.float32), *pairs], axis=1)
    return jnp.pad(out, ((0, 0), (0, fixed_width - out.shape[1]))).astype(jnp.bfloat16)


def moved_codes(moved, fixed, moved_width):
    every = jnp.concatenate([fixed, moved], axis=0)
    gram = jnp.einsum("ird,jrd->rij", moved, every, preferred_element_type=jnp.float32)
    pairs = [gram[:, i, : fixed.shape[0] + i] for i in range(moved.shape[0])]
    out = jnp.concatenate(pairs, axis=1)
    return jnp.pad(out, ((0, 0), (0, moved_width - out.shape[1]))).astype(jnp.bfloat16)


def top_kernel(in_width, codes_ref, weights_ref, out_w_ref, out_ref, acc_ref, codes_all_ref):
    step = pl.program_id(0)
    blk_width = weights_ref.shape[2]
    fixed_width = 2 * in_width - codes_ref.shape[2]

    @pl.when(step == 0)
    def _():
        codes = jnp.concatenate([codes_ref[x] for x in range(codes_ref.shape[0])], axis=0)
        rows = codes.shape[0]
        codes_all_ref[:rows] = codes[:, :in_width]
        codes_all_ref[rows:, :fixed_width] = codes[:, :fixed_width]
        codes_all_ref[rows:, fixed_width:] = codes[:, in_width:]
        acc_ref[...] = jnp.zeros_like(acc_ref)

    codes = codes_all_ref[...]
    hidden = []
    for blk in range(weights_ref.shape[0]):
        pre = jnp.dot(codes, weights_ref[blk, :in_width], preferred_element_type=jnp.float32)
        hidden.append(jnp.maximum(pre, 0.0).astype(jnp.bfloat16))
    for col in range(0, acc_ref.shape[1], blk_width):
        total = acc_ref[:, col : col + blk_width]
        row = in_width + col // blk_width * blk_width
        for blk in range(weights_ref.shape[0]):
            total += jnp.dot(
                hidden[blk],
                weights_ref[blk, row : row + blk_width],
                preferred_element_type=jnp.float32,
            )
        acc_ref[:, col : col + blk_width] = total

    @pl.when(step == pl.num_programs(0) - 1)
    def _():
        xs, variants, row_count = out_ref.shape
        scaled = jnp.maximum(acc_ref[...], 0.0) * out_w_ref[...]
        folded = scaled[:, :128]
        for lane in range(128, scaled.shape[1], 128):
            folded += scaled[:, lane : lane + 128]
        sums = jnp.sum(folded.T, axis=0, keepdims=True)
        for variant in range(variants):
            for x in range(xs):
                start = (variant * xs + x) * row_count
                out_ref[x, variant : variant + 1] = sums[:, start : start + row_count]


def top_layers(codes, weights, out_w, in_width):
    xs, row_count, _ = codes.shape
    groups, depth, blk_width = weights.shape
    steps = 2
    rows = 2 * xs * row_count
    return pl.pallas_call(
        functools.partial(top_kernel, in_width),
        grid=(steps,),
        in_specs=[
            pl.BlockSpec(memory_space=pltpu.VMEM),
            pl.BlockSpec((groups // steps, depth, blk_width), lambda i: (i, 0, 0)),
            pl.BlockSpec(memory_space=pltpu.VMEM),
        ],
        out_specs=pl.BlockSpec((xs, 2, row_count), lambda i: (0, 0, 0)),
        scratch_shapes=[
            pltpu.VMEM((rows, out_w.shape[1]), jnp.float32),
            pltpu.VMEM((rows, in_width), jnp.bfloat16),
        ],
        out_shape=jax.ShapeDtypeStruct((xs, 2, row_count), jnp.float32),
    )(codes, weights, out_w)


def local(
    dense_feats,
    sparse_ids,
    lengths,
    table_map,
    row_perm,
    tables,
    bottom_one,
    bottom_two,
    bottom_three,
    top_one,
    top_two,
    top_out,
):
    owners = lax.axis_size("tbl")
    owner_idx = lax.axis_index("tbl")
    xs = XS
    zs = owners // xs
    x_idx = owner_idx // zs
    along_x = [[x * zs + z for x in range(xs)] for z in range(zs)]
    out_cols = top_two.shape[1] // xs
    slot_count = tables.shape[0]
    row_count = dense_feats.shape[0]
    feats = sparse_ids.shape[0]
    dim = tables.shape[2]

    cols, fixed_width = code_order(feats, dim, top_one.shape[0])
    in_width = cols.shape[0]
    moved_width = in_width - fixed_width
    first_slot = (owner_idx * slot_count).astype(jnp.int32).reshape(1)
    pooled, packed = pool_slots(
        table_map,
        first_slot,
        x_idx.astype(jnp.int32).reshape(1),
        sparse_ids.transpose(0, 2, 1),
        lengths,
        tables,
        cols,
        top_one,
        top_two,
        (owners, row_count, out_cols),
    )
    weights = lax.all_gather(packed, "grp", axis=0, tiled=False)
    arrived = lax.all_to_all(pooled, "tbl", split_axis=0, concat_axis=0, tiled=True)
    arrived = arrived.reshape(owners * slot_count, row_count, dim)
    pick_slot = (
        table_map[:, None] == jnp.arange(owners * slot_count, dtype=jnp.int32)[None, :]
    ).astype(jnp.bfloat16)
    embedded = jnp.einsum(
        "fs,srd->frd", pick_slot, arrived, preferred_element_type=jnp.float32
    ).astype(jnp.bfloat16)

    bottom_out = dense_layer(
        dense_layer(dense_layer(dense_feats, bottom_one), bottom_two), bottom_three
    )
    gathered = lax.all_gather(embedded[:NPERM], "grp", axis=1, tiled=True)
    fixed = jnp.concatenate([bottom_out[None], embedded[NPERM:]], axis=0)
    code_fixed = fixed_codes(fixed, bottom_out, fixed_width)
    code_base = moved_codes(embedded[:NPERM], fixed, moved_width)
    source = row_perm // (owners * row_count) * row_count + row_perm % row_count
    pick_row = (source[:, None] == jnp.arange(gathered.shape[1], dtype=jnp.int32)[None, :]).astype(
        jnp.bfloat16
    )
    shuffled = jnp.einsum(
        "rs,psd->prd", pick_row, gathered, preferred_element_type=jnp.float32
    ).astype(jnp.bfloat16)
    code_perm = moved_codes(shuffled, fixed, moved_width)
    codes = jnp.concatenate([code_fixed, code_base, code_perm], axis=1)
    codes_all = lax.all_to_all(
        jnp.broadcast_to(codes[None], (xs, *codes.shape)),
        "tbl",
        split_axis=0,
        concat_axis=0,
        tiled=True,
        axis_index_groups=along_x,
    )
    out_w = lax.dynamic_slice(top_out, (x_idx * out_cols,), (out_cols,)).reshape(1, out_cols)
    part = top_layers(codes_all, weights, out_w.astype(jnp.float32), in_width)
    pieces = lax.all_to_all(
        part, "tbl", split_axis=0, concat_axis=0, tiled=True, axis_index_groups=along_x
    )
    return jax.nn.sigmoid(jnp.sum(pieces, axis=0))


def solution(mesh):
    placed = (
        P(("grp", "tbl"), None),
        P(None, "grp", None),
        P(None, "grp"),
        P(),
        P(("grp", "tbl")),
        P("tbl", None, None),
        P(),
        P(),
        P(),
        P(None, "grp"),
        P("grp", None),
        P(),
    )
    return jax.shard_map(
        local, mesh=mesh, in_specs=placed, out_specs=P(None, ("grp", "tbl")), check_vma=False
    )
```

```python
import functools

import jax
import jax.numpy as jnp
import numpy as np
from jax import lax
from jax.experimental import pallas as pl
from jax.experimental.pallas import tpu as pltpu
from jax.sharding import PartitionSpec as P

NPERM = 4
LO = 256
ROWBLK = 16
TILE = 512
XS = 4


def dense_layer(inputs, weights):
    return jnp.maximum(jnp.dot(inputs, weights, preferred_element_type=jnp.float32), 0.0).astype(
        jnp.bfloat16
    )


def spread_bags(ids):
    sub = lax.broadcasted_iota(jnp.int32, ids.shape, 0)
    grp = lax.broadcasted_iota(jnp.int32, ids.shape, 1) // ROWBLK
    for step in (1, 2, 4):
        down = pltpu.roll(pltpu.roll(ids, 8 - step, 0), ROWBLK * step, 1)
        up = pltpu.roll(pltpu.roll(ids, step, 0), 128 - ROWBLK * step, 1)
        sub_bit = (sub & step) != 0
        grp_bit = (grp & step) != 0
        ids = jnp.where(sub_bit == grp_bit, ids, jnp.where(sub_bit, up, down))
    return ids


def pack_loads(part_ref, one_ref, two_ref, first_ref, pack_ref, sems):
    depth, blk_width = two_ref.shape[0], one_ref.shape[1]
    count = sems.shape[0] - 2
    in_rows = pack_ref.shape[0] - count * depth
    loads = [pltpu.make_async_copy(one_ref, first_ref, sems.at[0])]
    for blk in range(count):
        start = pl.multiple_of((part_ref[0] * count + blk) * blk_width, blk_width)
        loads.append(
            pltpu.make_async_copy(
                two_ref.at[:, pl.ds(start, blk_width)],
                pack_ref.at[pl.ds(in_rows + blk * depth, depth)],
                sems.at[1 + blk],
            )
        )
    return loads


def pool_kernel(slot, map_ref, owner_ref, part_ref, ids_ref, len_ref, table_ref, *refs):
    packs = slot == 0
    cnt_ref, local_ref, sem = refs[-3:]
    if packs:
        cols_ref, one_ref, two_ref, out_ref, packed_ref, first_ref, pack_ref, sems = refs[:-3]
        loads = pack_loads(part_ref, one_ref, two_ref, first_ref, pack_ref, sems)
        for load in loads:
            load.start()
        send = pltpu.make_async_copy(pack_ref, packed_ref, sems.at[sems.shape[0] - 1])
    else:
        out_ref = refs[1]
    fetch = pltpu.make_async_copy(table_ref.at[slot], local_ref, sem)
    fetch.start()
    vocab = local_ref.shape[0]
    hi_count = vocab // LO
    height = hi_count * ROWBLK
    span = len_ref.shape[1]
    row_id = lax.broadcasted_iota(jnp.int32, (height, 128), 0)
    col_id = lax.broadcasted_iota(jnp.int32, (height, 128), 1)
    target = jnp.where(row_id % ROWBLK == col_id % ROWBLK, row_id // ROWBLK, -1)
    target = target.astype(jnp.float32).astype(jnp.bfloat16).reshape(-1, 16, 128)
    lo_id = lax.broadcasted_iota(jnp.int32, (LO, 128), 0)
    lo_id = lo_id.astype(jnp.float32).astype(jnp.bfloat16).reshape(-1, 16, 128)
    one = jnp.ones((), jnp.bfloat16)
    zero = jnp.zeros((), jnp.bfloat16)
    blank = jnp.zeros((height, 128), jnp.bfloat16)

    def one_hot(row, wanted):
        row = jnp.broadcast_to(row, (16, 128)).astype(jnp.bfloat16)
        return jnp.where(row[None] == wanted, one, zero).reshape(-1, 128)

    feat_pos = lax.broadcasted_iota(jnp.int32, len_ref.shape, 0)
    feat = find_feature(slot, map_ref, owner_ref)
    lens = jnp.sum(jnp.where(feat_pos == feat, len_ref[...], 0), axis=0, keepdims=True)
    for start in range(0, span, 128):
        ids = ids_ref[0, :, start : start + 128]
        bag_pos = lax.broadcasted_iota(jnp.int32, ids.shape, 0)
        ids = spread_bags(jnp.where(bag_pos < lens[:, start : start + 128], ids, vocab))
        high = (ids // LO).astype(jnp.float32)
        low = (ids % LO).astype(jnp.float32)
        for blk in range(0, 8, 2):
            lhs = [one_hot(high[i : i + 1], target) for i in (blk, blk + 1)]
            rhs = [one_hot(low[i : i + 1], lo_id) for i in (blk, blk + 1)]
            lhs = jnp.concatenate(
                [
                    jnp.concatenate([lhs[0], blank], axis=1),
                    jnp.concatenate([blank, lhs[1]], axis=1),
                ],
                axis=0,
            )
            counts = lax.dot_general(
                lhs,
                jnp.concatenate(rhs, axis=1),
                (((1,), (1,)), ((), ())),
                preferred_element_type=jnp.float32,
            ).astype(jnp.bfloat16)
            for part in range(2 * hi_count):
                row = start + (blk + part // hi_count) * ROWBLK
                col = part % hi_count * LO
                cnt_ref[row : row + ROWBLK, col : col + LO] = counts[
                    part * ROWBLK : (part + 1) * ROWBLK
                ]
        if packs and start == 0:
            for load in loads:
                load.wait()
            in_rows = cols_ref.shape[1]
            row = lax.broadcasted_iota(jnp.int32, (first_ref.shape[0], in_rows), 0)
            pick = jnp.where(row == cols_ref[...], 1.0, 0.0).astype(jnp.bfloat16)
            pack_ref[:in_rows] = lax.dot_general(
                pick, first_ref[...], (((0,), (0,)), ((), ())), preferred_element_type=jnp.float32
            ).astype(jnp.bfloat16)
            send.start()
    fetch.wait()
    row_count = out_ref.shape[2]
    for start in range(0, span, TILE):
        pooled = jnp.dot(
            cnt_ref[start : start + TILE], local_ref[...], preferred_element_type=jnp.float32
        ).astype(jnp.bfloat16)
        out_ref[start // row_count : (start + TILE) // row_count, 0] = pooled.reshape(
            TILE // row_count, row_count, out_ref.shape[3]
        )
    if packs:
        send.wait()


def find_feature(slot, map_ref, owner_ref):
    wanted = owner_ref[0] + slot
    feat = jnp.int32(0)
    for idx in range(map_ref.shape[0]):
        feat = jnp.where(map_ref[idx] == wanted, idx, feat)
    return feat


def pool_slots(
    table_map, first_slot, part, ids_t, lengths, tables, cols, top_one, top_two, dims
):
    owners, row_count, out_cols = dims
    slot_count, vocab, dim = tables.shape
    feats, bag, span = ids_t.shape
    blk_width = top_one.shape[1]
    count = out_cols // blk_width
    in_rows = cols.shape[0]
    packed_shape = (in_rows + count * top_two.shape[0], blk_width)
    pooled_shape = (owners, slot_count, row_count, dim)
    pooled_type = jax.ShapeDtypeStruct(pooled_shape, jnp.bfloat16)
    away = pl.BlockSpec(memory_space=pl.ANY)
    pooled = packed = None
    for slot in range(slot_count):
        in_specs = [
            pl.BlockSpec(
                (1, bag, span), lambda i, m, o, p, s=slot: (find_feature(s, m, o), 0, 0)
            ),
            pl.BlockSpec((feats, span), lambda i, m, o, p: (0, 0)),
            away,
        ]
        args = [table_map, first_slot, part, ids_t, lengths, tables]
        out_specs = [
            pl.BlockSpec(
                (owners, 1, row_count, dim), lambda i, m, o, p, s=slot: (0, s, 0, 0)
            )
        ]
        out_shape = [pooled_type]
        scratch = [
            pltpu.VMEM((span, vocab), jnp.bfloat16),
            pltpu.VMEM((vocab, dim), jnp.bfloat16),
            pltpu.SemaphoreType.DMA(()),
        ]
        aliases = {}
        if slot == 0:
            in_specs += [pl.BlockSpec((1, in_rows), lambda i, m, o, p: (0, 0)), away, away]
            args += [jnp.asarray(cols)[None], top_one, top_two]
            out_specs.append(away)
            out_shape.append(jax.ShapeDtypeStruct(packed_shape, jnp.bfloat16))
            scratch = [
                pltpu.VMEM(top_one.shape, jnp.bfloat16),
                pltpu.VMEM(packed_shape, jnp.bfloat16),
                pltpu.SemaphoreType.DMA((count + 2,)),
            ] + scratch
        else:
            in_specs.append(away)
            aliases = {len(args): 0}
            args.append(pooled)
        result = pl.pallas_call(
            functools.partial(pool_kernel, slot),
            grid_spec=pltpu.PrefetchScalarGridSpec(
                num_scalar_prefetch=3,
                grid=(1,),
                in_specs=in_specs,
                out_specs=out_specs,
                scratch_shapes=scratch,
            ),
            out_shape=out_shape,
            input_output_aliases=aliases,
        )(*args)
        pooled = result[0]
        if slot == 0:
            packed = result[1]
    return pooled, packed


def code_order(feats, dim, width):
    order = [0, *range(NPERM + 1, feats + 1), *range(1, NPERM + 1)]
    fixed = feats + 1 - NPERM

    def column(i, j):
        a, b = max(order[i], order[j]), min(order[i], order[j])
        return dim + a * (a - 1) // 2 + b

    cols = list(range(dim))
    cols += [column(i, j) for i in range(1, fixed) for j in range(i)]
    cols += [width - 1]
    cols += [-1] * (-len(cols) % 128)
    fixed_width = len(cols)
    cols += [column(i, j) for i in range(fixed, feats + 1) for j in range(i)]
    cols += [-1] * (-len(cols) % 128)
    return np.array(cols, np.int32), fixed_width


def fixed_codes(vectors, lead, fixed_width):
    gram = jnp.einsum("ird,jrd->rij", vectors, vectors, preferred_element_type=jnp.float32)
    pairs = [gram[:, level, :level] for level in range(1, vectors.shape[0])]
    out = jnp.concatenate([lead.astype(jnp.float32), *pairs], axis=1)
    return jnp.pad(out, ((0, 0), (0, fixed_width - out.shape[1]))).astype(jnp.bfloat16)


def moved_codes(moved, fixed, moved_width):
    every = jnp.concatenate([fixed, moved], axis=0)
    gram = jnp.einsum("ird,jrd->rij", moved, every, preferred_element_type=jnp.float32)
    pairs = [gram[:, i, : fixed.shape[0] + i] for i in range(moved.shape[0])]
    out = jnp.concatenate(pairs, axis=1)
    return jnp.pad(out, ((0, 0), (0, moved_width - out.shape[1]))).astype(jnp.bfloat16)


def top_kernel(in_width, codes_ref, weights_ref, out_w_ref, out_ref, acc_ref, codes_all_ref):
    step = pl.program_id(0)
    blk_width = weights_ref.shape[2]
    fixed_width = 2 * in_width - codes_ref.shape[2]

    @pl.when(step == 0)
    def _():
        codes = jnp.concatenate([codes_ref[x] for x in range(codes_ref.shape[0])], axis=0)
        rows = codes.shape[0]
        codes_all_ref[:rows] = codes[:, :in_width]
        codes_all_ref[rows:, :fixed_width] = codes[:, :fixed_width]
        codes_all_ref[rows:, fixed_width:] = codes[:, in_width:]
        acc_ref[...] = jnp.zeros_like(acc_ref)

    codes = codes_all_ref[...]
    hidden = []
    for blk in range(weights_ref.shape[0]):
        pre = jnp.dot(codes, weights_ref[blk, :in_width], preferred_element_type=jnp.float32)
        hidden.append(jnp.maximum(pre, 0.0).astype(jnp.bfloat16))
    for col in range(0, acc_ref.shape[1], blk_width):
        total = acc_ref[:, col : col + blk_width]
        row = weights_ref.shape[1] - acc_ref.shape[1] + col
        for blk in range(weights_ref.shape[0]):
            total += jnp.dot(
                hidden[blk],
                weights_ref[blk, row : row + blk_width],
                preferred_element_type=jnp.float32,
            )
        acc_ref[:, col : col + blk_width] = total

    @pl.when(step == pl.num_programs(0) - 1)
    def _():
        xs, variants, row_count = out_ref.shape
        scaled = jnp.maximum(acc_ref[...], 0.0) * out_w_ref[...]
        folded = scaled[:, :128]
        for lane in range(128, scaled.shape[1], 128):
            folded += scaled[:, lane : lane + 128]
        sums = jnp.sum(folded.T, axis=0, keepdims=True)
        for variant in range(variants):
            for x in range(xs):
                start = (variant * xs + x) * row_count
                out_ref[x, variant : variant + 1] = sums[:, start : start + row_count]


def top_layers(codes, weights, out_w, in_width):
    xs, row_count, _ = codes.shape
    groups, depth, blk_width = weights.shape
    steps = 2
    rows = 2 * xs * row_count
    return pl.pallas_call(
        functools.partial(top_kernel, in_width),
        grid=(steps,),
        in_specs=[
            pl.BlockSpec(memory_space=pltpu.VMEM),
            pl.BlockSpec((groups // steps, depth, blk_width), lambda i: (i, 0, 0)),
            pl.BlockSpec(memory_space=pltpu.VMEM),
        ],
        out_specs=pl.BlockSpec((xs, 2, row_count), lambda i: (0, 0, 0)),
        scratch_shapes=[
            pltpu.VMEM((rows, out_w.shape[1]), jnp.float32),
            pltpu.VMEM((rows, in_width), jnp.bfloat16),
        ],
        out_shape=jax.ShapeDtypeStruct((xs, 2, row_count), jnp.float32),
    )(codes, weights, out_w)


def local(
    dense_feats,
    sparse_ids,
    lengths,
    table_map,
    row_perm,
    tables,
    bottom_one,
    bottom_two,
    bottom_three,
    top_one,
    top_two,
    top_out,
):
    owners = lax.axis_size("tbl")
    owner_idx = lax.axis_index("tbl")
    xs = XS
    zs = owners // xs
    x_idx = owner_idx // zs
    along_x = [[x * zs + z for x in range(xs)] for z in range(zs)]
    out_cols = top_two.shape[1] // xs
    slot_count = tables.shape[0]
    row_count = dense_feats.shape[0]
    feats = sparse_ids.shape[0]
    dim = tables.shape[2]

    cols, fixed_width = code_order(feats, dim, top_one.shape[0])
    in_width = cols.shape[0]
    moved_width = in_width - fixed_width
    first_slot = (owner_idx * slot_count).astype(jnp.int32).reshape(1)
    pooled, packed = pool_slots(
        table_map,
        first_slot,
        x_idx.astype(jnp.int32).reshape(1),
        sparse_ids.transpose(0, 2, 1),
        lengths,
        tables,
        cols[: int(np.flatnonzero(cols >= 0)[-1]) // ROWBLK * ROWBLK + ROWBLK],
        top_one,
        top_two,
        (owners, row_count, out_cols),
    )
    weights = lax.all_gather(packed, "grp", axis=0, tiled=False)
    arrived = lax.all_to_all(pooled, "tbl", split_axis=0, concat_axis=0, tiled=True)
    arrived = arrived.reshape(owners * slot_count, row_count, dim)
    pick_slot = (
        table_map[:, None] == jnp.arange(owners * slot_count, dtype=jnp.int32)[None, :]
    ).astype(jnp.bfloat16)
    embedded = jnp.einsum(
        "fs,srd->frd", pick_slot, arrived, preferred_element_type=jnp.float32
    ).astype(jnp.bfloat16)

    bottom_out = dense_layer(
        dense_layer(dense_layer(dense_feats, bottom_one), bottom_two), bottom_three
    )
    gathered = lax.all_gather(embedded[:NPERM], "grp", axis=1, tiled=True)
    fixed = jnp.concatenate([bottom_out[None], embedded[NPERM:]], axis=0)
    code_fixed = fixed_codes(fixed, bottom_out, fixed_width)
    code_base = moved_codes(embedded[:NPERM], fixed, moved_width)
    source = row_perm // (owners * row_count) * row_count + row_perm % row_count
    pick_row = (source[:, None] == jnp.arange(gathered.shape[1], dtype=jnp.int32)[None, :]).astype(
        jnp.bfloat16
    )
    shuffled = jnp.einsum(
        "rs,psd->prd", pick_row, gathered, preferred_element_type=jnp.float32
    ).astype(jnp.bfloat16)
    code_perm = moved_codes(shuffled, fixed, moved_width)
    codes = jnp.concatenate([code_fixed, code_base, code_perm], axis=1)
    codes_all = lax.all_to_all(
        jnp.broadcast_to(codes[None], (xs, *codes.shape)),
        "tbl",
        split_axis=0,
        concat_axis=0,
        tiled=True,
        axis_index_groups=along_x,
    )
    out_w = lax.dynamic_slice(top_out, (x_idx * out_cols,), (out_cols,)).reshape(1, out_cols)
    part = top_layers(codes_all, weights, out_w.astype(jnp.float32), in_width)
    pieces = lax.all_to_all(
        part, "tbl", split_axis=0, concat_axis=0, tiled=True, axis_index_groups=along_x
    )
    return jax.nn.sigmoid(jnp.sum(pieces, axis=0))


def solution(mesh):
    placed = (
        P(("grp", "tbl"), None),
        P(None, "grp", None),
        P(None, "grp"),
        P(),
        P(("grp", "tbl")),
        P("tbl", None, None),
        P(),
        P(),
        P(),
        P(None, "grp"),
        P("grp", None),
        P(),
    )
    return jax.shard_map(
        local, mesh=mesh, in_specs=placed, out_specs=P(None, ("grp", "tbl")), check_vma=False
    )
```

```python
import jax
import jax.numpy as jnp
import numpy as np
from jax import lax
from jax.experimental import pallas as pl
from jax.experimental.pallas import tpu as pltpu
from jax.sharding import PartitionSpec as P

NPERM = 4
LO = 256
ROWBLK = 16
TILE = 512
XS = 4


def dense_layer(inputs, weights):
    return jnp.maximum(jnp.dot(inputs, weights, preferred_element_type=jnp.float32), 0.0).astype(
        jnp.bfloat16
    )


def spread_bags(ids):
    sub = lax.broadcasted_iota(jnp.int32, ids.shape, 0)
    grp = lax.broadcasted_iota(jnp.int32, ids.shape, 1) // ROWBLK
    for step in (1, 2, 4):
        down = pltpu.roll(pltpu.roll(ids, 8 - step, 0), ROWBLK * step, 1)
        up = pltpu.roll(pltpu.roll(ids, step, 0), 128 - ROWBLK * step, 1)
        sub_bit = (sub & step) != 0
        grp_bit = (grp & step) != 0
        ids = jnp.where(sub_bit == grp_bit, ids, jnp.where(sub_bit, up, down))
    return ids


def pool_kernel(map_ref, owner_ref, *refs):
    slot_count = len(refs) - 6
    ids_refs = refs[:slot_count]
    len_ref, table_ref, out_ref, cnt_ref, local_ref, sem = refs[slot_count:]
    vocab = table_ref.shape[1]
    hi_count = vocab // LO
    height = hi_count * ROWBLK
    span = len_ref.shape[1]
    fetch = pltpu.make_async_copy(table_ref, local_ref, sem)
    fetch.start()
    row_id = lax.broadcasted_iota(jnp.int32, (height, 128), 0)
    col_id = lax.broadcasted_iota(jnp.int32, (height, 128), 1)
    target = jnp.where(row_id % ROWBLK == col_id % ROWBLK, row_id // ROWBLK, -1)
    target = target.astype(jnp.float32).astype(jnp.bfloat16).reshape(-1, 16, 128)
    lo_id = lax.broadcasted_iota(jnp.int32, (LO, 128), 0)
    lo_id = lo_id.astype(jnp.float32).astype(jnp.bfloat16).reshape(-1, 16, 128)
    one = jnp.ones((), jnp.bfloat16)
    zero = jnp.zeros((), jnp.bfloat16)
    blank = jnp.zeros((height, 128), jnp.bfloat16)
    feat_pos = lax.broadcasted_iota(jnp.int32, len_ref.shape, 0)

    def one_hot(row, wanted):
        row = jnp.broadcast_to(row, (16, 128)).astype(jnp.bfloat16)
        return jnp.where(row[None] == wanted, one, zero).reshape(-1, 128)

    for slot in range(slot_count):
        feat = find_feature(slot, map_ref, owner_ref)
        lens = jnp.sum(jnp.where(feat_pos == feat, len_ref[...], 0), axis=0, keepdims=True)
        for start in range(0, span, 128):
            ids = ids_refs[slot][0, :, start : start + 128]
            bag_pos = lax.broadcasted_iota(jnp.int32, ids.shape, 0)
            ids = spread_bags(jnp.where(bag_pos < lens[:, start : start + 128], ids, vocab))
            high = (ids // LO).astype(jnp.float32)
            low = (ids % LO).astype(jnp.float32)
            for blk in range(0, 8, 2):
                lhs = [one_hot(high[i : i + 1], target) for i in (blk, blk + 1)]
                rhs = [one_hot(low[i : i + 1], lo_id) for i in (blk, blk + 1)]
                lhs = jnp.concatenate(
                    [
                        jnp.concatenate([lhs[0], blank], axis=1),
                        jnp.concatenate([blank, lhs[1]], axis=1),
                    ],
                    axis=0,
                )
                counts = lax.dot_general(
                    lhs,
                    jnp.concatenate(rhs, axis=1),
                    (((1,), (1,)), ((), ())),
                    preferred_element_type=jnp.float32,
                ).astype(jnp.bfloat16)
                for part in range(2 * hi_count):
                    row = start + (blk + part // hi_count) * ROWBLK
                    col = part % hi_count * LO
                    cnt_ref[slot, row : row + ROWBLK, col : col + LO] = counts[
                        part * ROWBLK : (part + 1) * ROWBLK
                    ]
        if slot == 0:
            fetch.wait()
        row_count = out_ref.shape[2]
        for start in range(0, span, TILE):
            pooled = jnp.dot(
                cnt_ref[slot, start : start + TILE],
                local_ref[slot],
                preferred_element_type=jnp.float32,
            ).astype(jnp.bfloat16)
            out_ref[start // row_count : (start + TILE) // row_count, slot] = pooled.reshape(
                TILE // row_count, row_count, out_ref.shape[3]
            )


def find_feature(slot, map_ref, owner_ref):
    wanted = owner_ref[0] + slot
    feat = jnp.int32(0)
    for idx in range(map_ref.shape[0]):
        feat = jnp.where(map_ref[idx] == wanted, idx, feat)
    return feat


def pool_slots(table_map, first_slot, ids_t, lengths, tables, owners, row_count):
    slot_count, vocab, dim = tables.shape
    feats, bag, span = ids_t.shape

    def ids_spec(slot):
        return pl.BlockSpec((1, bag, span), lambda i, m, o: (find_feature(slot, m, o), 0, 0))

    return pl.pallas_call(
        pool_kernel,
        grid_spec=pltpu.PrefetchScalarGridSpec(
            num_scalar_prefetch=2,
            grid=(1,),
            in_specs=[
                *[ids_spec(slot) for slot in range(slot_count)],
                pl.BlockSpec((feats, span), lambda i, m, o: (0, 0)),
                pl.BlockSpec(memory_space=pl.ANY),
            ],
            out_specs=pl.BlockSpec(
                (owners, slot_count, row_count, dim), lambda i, m, o: (0, 0, 0, 0)
            ),
            scratch_shapes=[
                pltpu.VMEM((slot_count, span, vocab), jnp.bfloat16),
                pltpu.VMEM(tables.shape, jnp.bfloat16),
                pltpu.SemaphoreType.DMA(()),
            ],
        ),
        out_shape=jax.ShapeDtypeStruct((owners, slot_count, row_count, dim), jnp.bfloat16),
    )(table_map, first_slot, *[ids_t] * slot_count, lengths, tables)


def pack_kernel(part_ref, one_ref, two_ref, out_ref, one_local_ref, two_local_ref, sems):
    in_rows, blk_width = one_ref.shape
    count, depth = two_local_ref.shape[:2]
    first = pltpu.make_async_copy(one_ref, one_local_ref, sems.at[0])
    loads = []
    sends = [pltpu.make_async_copy(one_local_ref, out_ref.at[pl.ds(0, in_rows)], sems.at[1])]
    for blk in range(count):
        start = pl.multiple_of((part_ref[0] * count + blk) * blk_width, blk_width)
        loads.append(
            pltpu.make_async_copy(
                two_ref.at[:, pl.ds(start, blk_width)], two_local_ref.at[blk], sems.at[2 + 2 * blk]
            )
        )
        sends.append(
            pltpu.make_async_copy(
                two_local_ref.at[blk],
                out_ref.at[pl.ds(in_rows + blk * depth, depth)],
                sems.at[3 + 2 * blk],
            )
        )
    loads.insert(0, first)
    for load in loads:
        load.start()
    for load, send in zip(loads, sends):
        load.wait()
        send.start()
    for send in sends:
        send.wait()


def pack_weights(part, top_one, top_two, out_cols):
    blk_width = top_one.shape[1]
    count = out_cols // blk_width
    depth = top_two.shape[0]
    away = pl.BlockSpec(memory_space=pl.ANY)
    return pl.pallas_call(
        pack_kernel,
        in_specs=[pl.BlockSpec(memory_space=pltpu.SMEM), away, away],
        out_specs=away,
        scratch_shapes=[
            pltpu.VMEM(top_one.shape, jnp.bfloat16),
            pltpu.VMEM((count, depth, blk_width), jnp.bfloat16),
            pltpu.SemaphoreType.DMA((2 + 2 * count,)),
        ],
        out_shape=jax.ShapeDtypeStruct((top_one.shape[0] + count * depth, blk_width), jnp.bfloat16),
    )(part.reshape(1), top_one, top_two)


def code_order(feats, dim, width):
    order = [0, *range(NPERM + 1, feats + 1), *range(1, NPERM + 1)]
    fixed = feats + 1 - NPERM

    def column(i, j):
        a, b = max(order[i], order[j]), min(order[i], order[j])
        return dim + a * (a - 1) // 2 + b

    cols = list(range(dim))
    cols += [column(i, j) for i in range(1, fixed) for j in range(i)]
    cols += [width - 1]
    cols += [-1] * (-len(cols) % 128)
    fixed_width = len(cols)
    cols += [column(i, j) for i in range(fixed, feats + 1) for j in range(i)]
    cols += [-1] * (-len(cols) % 128)
    return np.array(cols, np.int32), fixed_width


def fixed_codes(vectors, lead, fixed_width):
    gram = jnp.einsum("ird,jrd->rij", vectors, vectors, preferred_element_type=jnp.float32)
    pairs = [gram[:, level, :level] for level in range(1, vectors.shape[0])]
    out = jnp.concatenate([lead.astype(jnp.float32), *pairs], axis=1)
    return jnp.pad(out, ((0, 0), (0, fixed_width - out.shape[1]))).astype(jnp.bfloat16)


def moved_codes(moved, fixed, moved_width):
    every = jnp.concatenate([fixed, moved], axis=0)
    gram = jnp.einsum("ird,jrd->rij", moved, every, preferred_element_type=jnp.float32)
    pairs = [gram[:, i, : fixed.shape[0] + i] for i in range(moved.shape[0])]
    out = jnp.concatenate(pairs, axis=1)
    return jnp.pad(out, ((0, 0), (0, moved_width - out.shape[1]))).astype(jnp.bfloat16)


def top_kernel(codes_ref, cols_ref, weights_ref, out_w_ref, out_ref, acc_ref, codes_all_ref):
    step = pl.program_id(0)
    blk_width = weights_ref.shape[2]
    in_width = cols_ref.shape[1]
    in_rows = codes_all_ref.shape[1]
    fixed_width = 2 * in_width - codes_ref.shape[2]

    @pl.when(step == 0)
    def _():
        codes = jnp.concatenate([codes_ref[x] for x in range(codes_ref.shape[0])], axis=0)
        moved = jnp.concatenate([codes[:, :fixed_width], codes[:, in_width:]], axis=1)
        codes = jnp.concatenate([codes[:, :in_width], moved], axis=0)
        row = lax.broadcasted_iota(jnp.int32, (in_rows, in_width), 0)
        pick = jnp.where(row == cols_ref[...], 1.0, 0.0).astype(jnp.bfloat16)
        codes_all_ref[...] = lax.dot_general(
            codes, pick, (((1,), (1,)), ((), ())), preferred_element_type=jnp.float32
        ).astype(jnp.bfloat16)
        acc_ref[...] = jnp.zeros_like(acc_ref)

    codes = codes_all_ref[...]
    hidden = []
    for blk in range(weights_ref.shape[0]):
        pre = jnp.dot(codes, weights_ref[blk, :in_rows], preferred_element_type=jnp.float32)
        hidden.append(jnp.maximum(pre, 0.0).astype(jnp.bfloat16))
    for col in range(0, acc_ref.shape[1], blk_width):
        total = acc_ref[:, col : col + blk_width]
        row = in_rows + col
        for blk in range(weights_ref.shape[0]):
            total += jnp.dot(
                hidden[blk],
                weights_ref[blk, row : row + blk_width],
                preferred_element_type=jnp.float32,
            )
        acc_ref[:, col : col + blk_width] = total

    @pl.when(step == pl.num_programs(0) - 1)
    def _():
        xs, variants, row_count = out_ref.shape
        scaled = jnp.maximum(acc_ref[...], 0.0) * out_w_ref[...]
        folded = scaled[:, :128]
        for lane in range(128, scaled.shape[1], 128):
            folded += scaled[:, lane : lane + 128]
        sums = jnp.sum(folded.T, axis=0, keepdims=True)
        for variant in range(variants):
            for x in range(xs):
                start = (variant * xs + x) * row_count
                out_ref[x, variant : variant + 1] = sums[:, start : start + row_count]


def top_layers(codes, cols, weights, out_w):
    xs, row_count, _ = codes.shape
    groups, depth, blk_width = weights.shape
    steps = 2
    rows = 2 * xs * row_count
    return pl.pallas_call(
        top_kernel,
        grid=(steps,),
        in_specs=[
            pl.BlockSpec(memory_space=pltpu.VMEM),
            pl.BlockSpec(memory_space=pltpu.VMEM),
            pl.BlockSpec((groups // steps, depth, blk_width), lambda i: (i, 0, 0)),
            pl.BlockSpec(memory_space=pltpu.VMEM),
        ],
        out_specs=pl.BlockSpec((xs, 2, row_count), lambda i: (0, 0, 0)),
        scratch_shapes=[
            pltpu.VMEM((rows, out_w.shape[1]), jnp.float32),
            pltpu.VMEM((rows, depth - out_w.shape[1]), jnp.bfloat16),
        ],
        out_shape=jax.ShapeDtypeStruct((xs, 2, row_count), jnp.float32),
    )(codes, jnp.asarray(cols)[None], weights, out_w)


def local(
    dense_feats,
    sparse_ids,
    lengths,
    table_map,
    row_perm,
    tables,
    bottom_one,
    bottom_two,
    bottom_three,
    top_one,
    top_two,
    top_out,
):
    owners = lax.axis_size("tbl")
    owner_idx = lax.axis_index("tbl")
    xs = XS
    zs = owners // xs
    x_idx = owner_idx // zs
    along_x = [[x * zs + z for x in range(xs)] for z in range(zs)]
    out_cols = top_two.shape[1] // xs
    slot_count = tables.shape[0]
    row_count = dense_feats.shape[0]
    feats = sparse_ids.shape[0]
    dim = tables.shape[2]

    cols, fixed_width = code_order(feats, dim, top_one.shape[0])
    in_width = cols.shape[0]
    moved_width = in_width - fixed_width
    packed = pack_weights(x_idx.astype(jnp.int32), top_one, top_two, out_cols)
    weights = lax.all_gather(packed, "grp", axis=0, tiled=False)

    first_slot = (owner_idx * slot_count).astype(jnp.int32).reshape(1)
    pooled = pool_slots(
        table_map, first_slot, sparse_ids.transpose(0, 2, 1), lengths, tables, owners, row_count
    )
    arrived = lax.all_to_all(pooled, "tbl", split_axis=0, concat_axis=0, tiled=True)
    arrived = arrived.reshape(owners * slot_count, row_count, dim)
    pick_slot = (
        table_map[:, None] == jnp.arange(owners * slot_count, dtype=jnp.int32)[None, :]
    ).astype(jnp.bfloat16)
    embedded = jnp.einsum(
        "fs,srd->frd", pick_slot, arrived, preferred_element_type=jnp.float32
    ).astype(jnp.bfloat16)

    bottom_out = dense_layer(
        dense_layer(dense_layer(dense_feats, bottom_one), bottom_two), bottom_three
    )
    gathered = lax.all_gather(embedded[:NPERM], "grp", axis=1, tiled=True)
    fixed = jnp.concatenate([bottom_out[None], embedded[NPERM:]], axis=0)
    code_fixed = fixed_codes(fixed, bottom_out, fixed_width)
    code_base = moved_codes(embedded[:NPERM], fixed, moved_width)
    source = row_perm // (owners * row_count) * row_count + row_perm % row_count
    pick_row = (source[:, None] == jnp.arange(gathered.shape[1], dtype=jnp.int32)[None, :]).astype(
        jnp.bfloat16
    )
    shuffled = jnp.einsum(
        "rs,psd->prd", pick_row, gathered, preferred_element_type=jnp.float32
    ).astype(jnp.bfloat16)
    code_perm = moved_codes(shuffled, fixed, moved_width)
    codes = jnp.concatenate([code_fixed, code_base, code_perm], axis=1)
    codes_all = lax.all_to_all(
        jnp.broadcast_to(codes[None], (xs, *codes.shape)),
        "tbl",
        split_axis=0,
        concat_axis=0,
        tiled=True,
        axis_index_groups=along_x,
    )
    out_w = lax.dynamic_slice(top_out, (x_idx * out_cols,), (out_cols,)).reshape(1, out_cols)
    codes_all = pltpu.with_memory_space_constraint(codes_all, pltpu.VMEM)
    part = top_layers(codes_all, cols, weights, out_w.astype(jnp.float32))
    pieces = lax.all_to_all(
        part, "tbl", split_axis=0, concat_axis=0, tiled=True, axis_index_groups=along_x
    )
    return jax.nn.sigmoid(jnp.sum(pieces, axis=0))


def solution(mesh):
    placed = (
        P(("grp", "tbl"), None),
        P(None, "grp", None),
        P(None, "grp"),
        P(),
        P(("grp", "tbl")),
        P("tbl", None, None),
        P(),
        P(),
        P(),
        P(None, "grp"),
        P("grp", None),
        P(),
    )
    return jax.shard_map(
        local, mesh=mesh, in_specs=placed, out_specs=P(None, ("grp", "tbl")), check_vma=False
    )
```

```python
import jax
import jax.numpy as jnp
import numpy as np
from jax import lax
from jax.experimental import pallas as pl
from jax.experimental.pallas import tpu as pltpu
from jax.sharding import PartitionSpec as P

NPERM = 4
LO = 256
ROWBLK = 16
TILE = 512
XS = 4


def dense_layer(inputs, weights):
    return jnp.maximum(jnp.dot(inputs, weights, preferred_element_type=jnp.float32), 0.0).astype(
        jnp.bfloat16
    )


def spread_bags(ids):
    sub = lax.broadcasted_iota(jnp.int32, ids.shape, 0)
    grp = lax.broadcasted_iota(jnp.int32, ids.shape, 1) // ROWBLK
    for step in (1, 2, 4):
        down = pltpu.roll(pltpu.roll(ids, 8 - step, 0), ROWBLK * step, 1)
        up = pltpu.roll(pltpu.roll(ids, step, 0), 128 - ROWBLK * step, 1)
        sub_bit = (sub & step) != 0
        grp_bit = (grp & step) != 0
        ids = jnp.where(sub_bit == grp_bit, ids, jnp.where(sub_bit, up, down))
    return ids


def pool_kernel(map_ref, owner_ref, *refs):
    slot_count = len(refs) - 8
    ids_refs = refs[:slot_count]
    len_ref, table_ref, out_ref, cnt_ref, local_ref, rows_ref, sem, sems = refs[slot_count:]
    vocab = table_ref.shape[1]
    hi_count = vocab // LO
    height = hi_count * ROWBLK
    span = len_ref.shape[1]
    fetch = pltpu.make_async_copy(table_ref, local_ref, sem)
    fetch.start()
    row_id = lax.broadcasted_iota(jnp.int32, (height, 128), 0)
    col_id = lax.broadcasted_iota(jnp.int32, (height, 128), 1)
    target = jnp.where(row_id % ROWBLK == col_id % ROWBLK, row_id // ROWBLK, -1)
    target = target.astype(jnp.float32).astype(jnp.bfloat16).reshape(-1, 16, 128)
    lo_id = lax.broadcasted_iota(jnp.int32, (LO, 128), 0)
    lo_id = lo_id.astype(jnp.float32).astype(jnp.bfloat16).reshape(-1, 16, 128)
    one = jnp.ones((), jnp.bfloat16)
    zero = jnp.zeros((), jnp.bfloat16)
    blank = jnp.zeros((height, 128), jnp.bfloat16)
    feat_pos = lax.broadcasted_iota(jnp.int32, len_ref.shape, 0)

    def one_hot(row, wanted):
        row = jnp.broadcast_to(row, (16, 128)).astype(jnp.bfloat16)
        return jnp.where(row[None] == wanted, one, zero).reshape(-1, 128)

    sends = []
    for slot in range(slot_count):
        feat = find_feature(slot, map_ref, owner_ref)
        lens = jnp.sum(jnp.where(feat_pos == feat, len_ref[...], 0), axis=0, keepdims=True)
        for start in range(0, span, 128):
            ids = ids_refs[slot][0, :, start : start + 128]
            bag_pos = lax.broadcasted_iota(jnp.int32, ids.shape, 0)
            ids = spread_bags(jnp.where(bag_pos < lens[:, start : start + 128], ids, vocab))
            high = (ids // LO).astype(jnp.float32)
            low = (ids % LO).astype(jnp.float32)
            for blk in range(0, 8, 2):
                lhs = [one_hot(high[i : i + 1], target) for i in (blk, blk + 1)]
                rhs = [one_hot(low[i : i + 1], lo_id) for i in (blk, blk + 1)]
                lhs = jnp.concatenate(
                    [
                        jnp.concatenate([lhs[0], blank], axis=1),
                        jnp.concatenate([blank, lhs[1]], axis=1),
                    ],
                    axis=0,
                )
                counts = lax.dot_general(
                    lhs,
                    jnp.concatenate(rhs, axis=1),
                    (((1,), (1,)), ((), ())),
                    preferred_element_type=jnp.float32,
                ).astype(jnp.bfloat16)
                for part in range(2 * hi_count):
                    row = start + (blk + part // hi_count) * ROWBLK
                    col = part % hi_count * LO
                    cnt_ref[slot, row : row + ROWBLK, col : col + LO] = counts[
                        part * ROWBLK : (part + 1) * ROWBLK
                    ]
        if slot == 0:
            fetch.wait()
        row_count = out_ref.shape[2]
        for start in range(0, span, TILE):
            pooled = jnp.dot(
                cnt_ref[slot, start : start + TILE],
                local_ref[slot],
                preferred_element_type=jnp.float32,
            ).astype(jnp.bfloat16)
            first, last = start // row_count, (start + TILE) // row_count
            rows_ref[slot, first:last] = pooled.reshape(last - first, row_count, out_ref.shape[3])
        sends.append(pltpu.make_async_copy(rows_ref.at[slot], out_ref.at[:, slot], sems.at[slot]))
        sends[-1].start()
    for send in sends:
        send.wait()


def find_feature(slot, map_ref, owner_ref):
    wanted = owner_ref[0] + slot
    feat = jnp.int32(0)
    for idx in range(map_ref.shape[0]):
        feat = jnp.where(map_ref[idx] == wanted, idx, feat)
    return feat


def pool_slots(table_map, first_slot, ids_t, lengths, tables, owners, row_count):
    slot_count, vocab, dim = tables.shape
    feats, bag, span = ids_t.shape

    def ids_spec(slot):
        return pl.BlockSpec((1, bag, span), lambda i, m, o: (find_feature(slot, m, o), 0, 0))

    return pl.pallas_call(
        pool_kernel,
        grid_spec=pltpu.PrefetchScalarGridSpec(
            num_scalar_prefetch=2,
            grid=(1,),
            in_specs=[
                *[ids_spec(slot) for slot in range(slot_count)],
                pl.BlockSpec((feats, span), lambda i, m, o: (0, 0)),
                pl.BlockSpec(memory_space=pl.ANY),
            ],
            out_specs=pl.BlockSpec(memory_space=pl.ANY),
            scratch_shapes=[
                pltpu.VMEM((slot_count, span, vocab), jnp.bfloat16),
                pltpu.VMEM(tables.shape, jnp.bfloat16),
                pltpu.VMEM((slot_count, owners, row_count, dim), jnp.bfloat16),
                pltpu.SemaphoreType.DMA(()),
                pltpu.SemaphoreType.DMA((slot_count,)),
            ],
        ),
        out_shape=jax.ShapeDtypeStruct((owners, slot_count, row_count, dim), jnp.bfloat16),
    )(table_map, first_slot, *[ids_t] * slot_count, lengths, tables)


def pack_kernel(part_ref, one_ref, two_ref, out_ref, one_local_ref, two_local_ref, sems):
    in_rows, blk_width = one_ref.shape
    count, depth = two_local_ref.shape[:2]
    first = pltpu.make_async_copy(one_ref, one_local_ref, sems.at[0])
    loads = []
    sends = [pltpu.make_async_copy(one_local_ref, out_ref.at[pl.ds(0, in_rows)], sems.at[1])]
    for blk in range(count):
        start = pl.multiple_of((part_ref[0] * count + blk) * blk_width, blk_width)
        loads.append(
            pltpu.make_async_copy(
                two_ref.at[:, pl.ds(start, blk_width)], two_local_ref.at[blk], sems.at[2 + 2 * blk]
            )
        )
        sends.append(
            pltpu.make_async_copy(
                two_local_ref.at[blk],
                out_ref.at[pl.ds(in_rows + blk * depth, depth)],
                sems.at[3 + 2 * blk],
            )
        )
    loads.insert(0, first)
    for load in loads:
        load.start()
    for load, send in zip(loads, sends):
        load.wait()
        send.start()
    for send in sends:
        send.wait()


def pack_weights(part, top_one, top_two, out_cols):
    blk_width = top_one.shape[1]
    count = out_cols // blk_width
    depth = top_two.shape[0]
    away = pl.BlockSpec(memory_space=pl.ANY)
    return pl.pallas_call(
        pack_kernel,
        in_specs=[pl.BlockSpec(memory_space=pltpu.SMEM), away, away],
        out_specs=away,
        scratch_shapes=[
            pltpu.VMEM(top_one.shape, jnp.bfloat16),
            pltpu.VMEM((count, depth, blk_width), jnp.bfloat16),
            pltpu.SemaphoreType.DMA((2 + 2 * count,)),
        ],
        out_shape=jax.ShapeDtypeStruct((top_one.shape[0] + count * depth, blk_width), jnp.bfloat16),
    )(part.reshape(1), top_one, top_two)


def select_kernel(map_ref, arrived_ref, moved_ref, kept_ref):
    moved = moved_ref.shape[0]
    for feat in range(map_ref.shape[0]):
        value = arrived_ref[map_ref[feat]]
        if feat < moved:
            moved_ref[feat] = value
        else:
            kept_ref[feat - moved] = value


def select_slots(table_map, arrived):
    feats = table_map.shape[0]
    whole = pl.BlockSpec(memory_space=pltpu.VMEM)
    return pl.pallas_call(
        select_kernel,
        in_specs=[pl.BlockSpec(memory_space=pltpu.SMEM), whole],
        out_specs=[whole, whole],
        out_shape=[
            jax.ShapeDtypeStruct((NPERM, *arrived.shape[1:]), arrived.dtype),
            jax.ShapeDtypeStruct((feats - NPERM, *arrived.shape[1:]), arrived.dtype),
        ],
    )(table_map, pltpu.with_memory_space_constraint(arrived, pltpu.VMEM))


def code_order(feats, dim, width):
    order = [0, *range(NPERM + 1, feats + 1), *range(1, NPERM + 1)]
    fixed = feats + 1 - NPERM

    def column(i, j):
        a, b = max(order[i], order[j]), min(order[i], order[j])
        return dim + a * (a - 1) // 2 + b

    cols = list(range(dim))
    cols += [column(i, j) for i in range(1, fixed) for j in range(i)]
    cols += [width - 1]
    cols += [-1] * (-len(cols) % 128)
    fixed_width = len(cols)
    cols += [column(i, j) for i in range(fixed, feats + 1) for j in range(i)]
    cols += [-1] * (-len(cols) % 128)
    return np.array(cols, np.int32), fixed_width


def fixed_codes(vectors, lead, fixed_width):
    gram = jnp.einsum("ird,jrd->rij", vectors, vectors, preferred_element_type=jnp.float32)
    pairs = [gram[:, level, :level] for level in range(1, vectors.shape[0])]
    out = jnp.concatenate([lead.astype(jnp.float32), *pairs], axis=1)
    return jnp.pad(out, ((0, 0), (0, fixed_width - out.shape[1]))).astype(jnp.bfloat16)


def moved_codes(moved, fixed, moved_width):
    every = jnp.concatenate([fixed, moved], axis=0)
    gram = jnp.einsum("ird,jrd->rij", moved, every, preferred_element_type=jnp.float32)
    pairs = [gram[:, i, : fixed.shape[0] + i] for i in range(moved.shape[0])]
    out = jnp.concatenate(pairs, axis=1)
    return jnp.pad(out, ((0, 0), (0, moved_width - out.shape[1]))).astype(jnp.bfloat16)


def top_kernel(codes_ref, cols_ref, weights_ref, out_w_ref, out_ref, acc_ref, codes_all_ref):
    step = pl.program_id(0)
    blk_width = weights_ref.shape[2]
    in_width = cols_ref.shape[1]
    in_rows = codes_all_ref.shape[1]
    fixed_width = 2 * in_width - codes_ref.shape[2]

    @pl.when(step == 0)
    def _():
        codes = jnp.concatenate([codes_ref[x] for x in range(codes_ref.shape[0])], axis=0)
        moved = jnp.concatenate([codes[:, :fixed_width], codes[:, in_width:]], axis=1)
        codes = jnp.concatenate([codes[:, :in_width], moved], axis=0)
        row = lax.broadcasted_iota(jnp.int32, (in_rows, in_width), 0)
        pick = jnp.where(row == cols_ref[...], 1.0, 0.0).astype(jnp.bfloat16)
        codes_all_ref[...] = lax.dot_general(
            codes, pick, (((1,), (1,)), ((), ())), preferred_element_type=jnp.float32
        ).astype(jnp.bfloat16)
        acc_ref[...] = jnp.zeros_like(acc_ref)

    codes = codes_all_ref[...]
    hidden = []
    for blk in range(weights_ref.shape[0]):
        pre = jnp.dot(codes, weights_ref[blk, :in_rows], preferred_element_type=jnp.float32)
        hidden.append(jnp.maximum(pre, 0.0).astype(jnp.bfloat16))
    for col in range(0, acc_ref.shape[1], blk_width):
        total = acc_ref[:, col : col + blk_width]
        row = in_rows + col
        for blk in range(weights_ref.shape[0]):
            total += jnp.dot(
                hidden[blk],
                weights_ref[blk, row : row + blk_width],
                preferred_element_type=jnp.float32,
            )
        acc_ref[:, col : col + blk_width] = total

    @pl.when(step == pl.num_programs(0) - 1)
    def _():
        xs, variants, row_count = out_ref.shape
        scaled = jnp.maximum(acc_ref[...], 0.0) * out_w_ref[...]
        folded = scaled[:, :128]
        for lane in range(128, scaled.shape[1], 128):
            folded += scaled[:, lane : lane + 128]
        sums = jnp.sum(folded.T, axis=0, keepdims=True)
        for variant in range(variants):
            for x in range(xs):
                start = (variant * xs + x) * row_count
                out_ref[x, variant : variant + 1] = sums[:, start : start + row_count]


def top_layers(codes, cols, weights, out_w):
    xs, row_count, _ = codes.shape
    groups, depth, blk_width = weights.shape
    steps = 2
    rows = 2 * xs * row_count
    return pl.pallas_call(
        top_kernel,
        grid=(steps,),
        in_specs=[
            pl.BlockSpec(memory_space=pltpu.VMEM),
            pl.BlockSpec(memory_space=pltpu.VMEM),
            pl.BlockSpec((groups // steps, depth, blk_width), lambda i: (i, 0, 0)),
            pl.BlockSpec(memory_space=pltpu.VMEM),
        ],
        out_specs=pl.BlockSpec((xs, 2, row_count), lambda i: (0, 0, 0)),
        scratch_shapes=[
            pltpu.VMEM((rows, out_w.shape[1]), jnp.float32),
            pltpu.VMEM((rows, depth - out_w.shape[1]), jnp.bfloat16),
        ],
        out_shape=jax.ShapeDtypeStruct((xs, 2, row_count), jnp.float32),
    )(codes, jnp.asarray(cols)[None], weights, out_w)


def local(
    dense_feats,
    sparse_ids,
    lengths,
    table_map,
    row_perm,
    tables,
    bottom_one,
    bottom_two,
    bottom_three,
    top_one,
    top_two,
    top_out,
):
    owners = lax.axis_size("tbl")
    owner_idx = lax.axis_index("tbl")
    xs = XS
    zs = owners // xs
    x_idx = owner_idx // zs
    along_x = [[x * zs + z for x in range(xs)] for z in range(zs)]
    out_cols = top_two.shape[1] // xs
    slot_count = tables.shape[0]
    row_count = dense_feats.shape[0]
    feats = sparse_ids.shape[0]
    dim = tables.shape[2]

    cols, fixed_width = code_order(feats, dim, top_one.shape[0])
    in_width = cols.shape[0]
    moved_width = in_width - fixed_width
    packed = pack_weights(x_idx.astype(jnp.int32), top_one, top_two, out_cols)
    weights = lax.all_gather(packed, "grp", axis=0, tiled=False)

    first_slot = (owner_idx * slot_count).astype(jnp.int32).reshape(1)
    pooled = pool_slots(
        table_map, first_slot, sparse_ids.transpose(0, 2, 1), lengths, tables, owners, row_count
    )
    arrived = lax.all_to_all(pooled, "tbl", split_axis=0, concat_axis=0, tiled=True)
    arrived = arrived.reshape(owners * slot_count, row_count, dim)
    moved, kept = select_slots(table_map, arrived)

    bottom_out = dense_layer(
        dense_layer(dense_layer(dense_feats, bottom_one), bottom_two), bottom_three
    )
    gathered = lax.all_gather(moved, "grp", axis=1, tiled=True)
    fixed = jnp.concatenate([bottom_out[None], kept], axis=0)
    code_fixed = fixed_codes(fixed, bottom_out, fixed_width)
    code_base = moved_codes(moved, fixed, moved_width)
    source = row_perm // (owners * row_count) * row_count + row_perm % row_count
    pick_row = (source[:, None] == jnp.arange(gathered.shape[1], dtype=jnp.int32)[None, :]).astype(
        jnp.bfloat16
    )
    shuffled = jnp.einsum(
        "rs,psd->prd", pick_row, gathered, preferred_element_type=jnp.float32
    ).astype(jnp.bfloat16)
    code_perm = moved_codes(shuffled, fixed, moved_width)
    codes = jnp.concatenate([code_fixed, code_base, code_perm], axis=1)
    codes_all = lax.all_to_all(
        jnp.broadcast_to(codes[None], (xs, *codes.shape)),
        "tbl",
        split_axis=0,
        concat_axis=0,
        tiled=True,
        axis_index_groups=along_x,
    )
    out_w = lax.dynamic_slice(top_out, (x_idx * out_cols,), (out_cols,)).reshape(1, out_cols)
    codes_all = pltpu.with_memory_space_constraint(codes_all, pltpu.VMEM)
    part = top_layers(codes_all, cols, weights, out_w.astype(jnp.float32))
    pieces = lax.all_to_all(
        part, "tbl", split_axis=0, concat_axis=0, tiled=True, axis_index_groups=along_x
    )
    return jax.nn.sigmoid(jnp.sum(pieces, axis=0))


def solution(mesh):
    placed = (
        P(("grp", "tbl"), None),
        P(None, "grp", None),
        P(None, "grp"),
        P(),
        P(("grp", "tbl")),
        P("tbl", None, None),
        P(),
        P(),
        P(),
        P(None, "grp"),
        P("grp", None),
        P(),
    )
    return jax.shard_map(
        local, mesh=mesh, in_specs=placed, out_specs=P(None, ("grp", "tbl")), check_vma=False
    )
```

```python
import jax
import jax.numpy as jnp
import numpy as np
from jax import lax
from jax.experimental import pallas as pl
from jax.experimental.pallas import tpu as pltpu
from jax.sharding import PartitionSpec as P

NPERM = 4
LO = 256
ROWBLK = 16
TILE = 512
XS = 4


def dense_layer(inputs, weights):
    return jnp.maximum(jnp.dot(inputs, weights, preferred_element_type=jnp.float32), 0.0).astype(
        jnp.bfloat16
    )


def spread_bags(ids):
    sub = lax.broadcasted_iota(jnp.int32, ids.shape, 0)
    grp = lax.broadcasted_iota(jnp.int32, ids.shape, 1) // ROWBLK
    for step in (1, 2, 4):
        down = pltpu.roll(pltpu.roll(ids, 8 - step, 0), ROWBLK * step, 1)
        up = pltpu.roll(pltpu.roll(ids, step, 0), 128 - ROWBLK * step, 1)
        sub_bit = (sub & step) != 0
        grp_bit = (grp & step) != 0
        ids = jnp.where(sub_bit == grp_bit, ids, jnp.where(sub_bit, up, down))
    return ids


def pool_kernel(map_ref, owner_ref, *refs):
    slot_count = len(refs) - 8
    ids_refs = refs[:slot_count]
    len_ref, table_ref, out_ref, cnt_ref, local_ref, rows_ref, sem, sems = refs[slot_count:]
    vocab = table_ref.shape[1]
    hi_count = vocab // LO
    height = hi_count * ROWBLK
    span = len_ref.shape[1]
    fetch = pltpu.make_async_copy(table_ref, local_ref, sem)
    fetch.start()
    row_id = lax.broadcasted_iota(jnp.int32, (height, 128), 0)
    col_id = lax.broadcasted_iota(jnp.int32, (height, 128), 1)
    target = jnp.where(row_id % ROWBLK == col_id % ROWBLK, row_id // ROWBLK, -1)
    target = target.astype(jnp.float32).astype(jnp.bfloat16).reshape(-1, 16, 128)
    lo_id = lax.broadcasted_iota(jnp.int32, (LO, 128), 0)
    lo_id = lo_id.astype(jnp.float32).astype(jnp.bfloat16).reshape(-1, 16, 128)
    one = jnp.ones((), jnp.bfloat16)
    zero = jnp.zeros((), jnp.bfloat16)
    blank = jnp.zeros((height, 128), jnp.bfloat16)
    feat_pos = lax.broadcasted_iota(jnp.int32, len_ref.shape, 0)

    def one_hot(row, wanted):
        row = jnp.broadcast_to(row, (16, 128)).astype(jnp.bfloat16)
        return jnp.where(row[None] == wanted, one, zero).reshape(-1, 128)

    sends = []
    for slot in range(slot_count):
        feat = find_feature(slot, map_ref, owner_ref)
        lens = jnp.sum(jnp.where(feat_pos == feat, len_ref[...], 0), axis=0, keepdims=True)
        for start in range(0, span, 128):
            ids = ids_refs[slot][0, :, start : start + 128]
            bag_pos = lax.broadcasted_iota(jnp.int32, ids.shape, 0)
            ids = spread_bags(jnp.where(bag_pos < lens[:, start : start + 128], ids, vocab))
            high = (ids // LO).astype(jnp.float32)
            low = (ids % LO).astype(jnp.float32)
            for blk in range(0, 8, 2):
                lhs = [one_hot(high[i : i + 1], target) for i in (blk, blk + 1)]
                rhs = [one_hot(low[i : i + 1], lo_id) for i in (blk, blk + 1)]
                lhs = jnp.concatenate(
                    [
                        jnp.concatenate([lhs[0], blank], axis=1),
                        jnp.concatenate([blank, lhs[1]], axis=1),
                    ],
                    axis=0,
                )
                counts = lax.dot_general(
                    lhs,
                    jnp.concatenate(rhs, axis=1),
                    (((1,), (1,)), ((), ())),
                    preferred_element_type=jnp.float32,
                ).astype(jnp.bfloat16)
                for part in range(2 * hi_count):
                    row = start + (blk + part // hi_count) * ROWBLK
                    col = part % hi_count * LO
                    cnt_ref[slot, row : row + ROWBLK, col : col + LO] = counts[
                        part * ROWBLK : (part + 1) * ROWBLK
                    ]
        if slot == 0:
            fetch.wait()
        row_count = out_ref.shape[2]
        for start in range(0, span, TILE):
            pooled = jnp.dot(
                cnt_ref[slot, start : start + TILE],
                local_ref[slot],
                preferred_element_type=jnp.float32,
            ).astype(jnp.bfloat16)
            first, last = start // row_count, (start + TILE) // row_count
            rows_ref[slot, first:last] = pooled.reshape(last - first, row_count, out_ref.shape[3])
        sends.append(pltpu.make_async_copy(rows_ref.at[slot], out_ref.at[:, slot], sems.at[slot]))
        sends[-1].start()
    for send in sends:
        send.wait()


def find_feature(slot, map_ref, owner_ref):
    wanted = owner_ref[0] + slot
    feat = jnp.int32(0)
    for idx in range(map_ref.shape[0]):
        feat = jnp.where(map_ref[idx] == wanted, idx, feat)
    return feat


def pool_slots(table_map, first_slot, ids_t, lengths, tables, owners, row_count):
    slot_count, vocab, dim = tables.shape
    feats, bag, span = ids_t.shape

    def ids_spec(slot):
        return pl.BlockSpec((1, bag, span), lambda i, m, o: (find_feature(slot, m, o), 0, 0))

    return pl.pallas_call(
        pool_kernel,
        grid_spec=pltpu.PrefetchScalarGridSpec(
            num_scalar_prefetch=2,
            grid=(1,),
            in_specs=[
                *[ids_spec(slot) for slot in range(slot_count)],
                pl.BlockSpec((feats, span), lambda i, m, o: (0, 0)),
                pl.BlockSpec(memory_space=pl.ANY),
            ],
            out_specs=pl.BlockSpec(memory_space=pl.ANY),
            scratch_shapes=[
                pltpu.VMEM((slot_count, span, vocab), jnp.bfloat16),
                pltpu.VMEM(tables.shape, jnp.bfloat16),
                pltpu.VMEM((slot_count, owners, row_count, dim), jnp.bfloat16),
                pltpu.SemaphoreType.DMA(()),
                pltpu.SemaphoreType.DMA((slot_count,)),
            ],
        ),
        out_shape=jax.ShapeDtypeStruct((owners, slot_count, row_count, dim), jnp.bfloat16),
    )(table_map, first_slot, *[ids_t] * slot_count, lengths, tables)


def pack_kernel(part_ref, one_ref, two_ref, out_ref, one_local_ref, two_local_ref, sems):
    in_rows, blk_width = one_ref.shape
    count, depth = two_local_ref.shape[:2]
    first = pltpu.make_async_copy(one_ref, one_local_ref, sems.at[0])
    loads = []
    sends = [pltpu.make_async_copy(one_local_ref, out_ref.at[pl.ds(0, in_rows)], sems.at[1])]
    for blk in range(count):
        start = pl.multiple_of((part_ref[0] * count + blk) * blk_width, blk_width)
        loads.append(
            pltpu.make_async_copy(
                two_ref.at[:, pl.ds(start, blk_width)], two_local_ref.at[blk], sems.at[2 + 2 * blk]
            )
        )
        sends.append(
            pltpu.make_async_copy(
                two_local_ref.at[blk],
                out_ref.at[pl.ds(in_rows + blk * depth, depth)],
                sems.at[3 + 2 * blk],
            )
        )
    loads.insert(0, first)
    for load in loads:
        load.start()
    for load, send in zip(loads, sends):
        load.wait()
        send.start()
    for send in sends:
        send.wait()


def pack_weights(part, top_one, top_two, out_cols):
    blk_width = top_one.shape[1]
    count = out_cols // blk_width
    depth = top_two.shape[0]
    away = pl.BlockSpec(memory_space=pl.ANY)
    return pl.pallas_call(
        pack_kernel,
        in_specs=[pl.BlockSpec(memory_space=pltpu.SMEM), away, away],
        out_specs=away,
        scratch_shapes=[
            pltpu.VMEM(top_one.shape, jnp.bfloat16),
            pltpu.VMEM((count, depth, blk_width), jnp.bfloat16),
            pltpu.SemaphoreType.DMA((2 + 2 * count,)),
        ],
        out_shape=jax.ShapeDtypeStruct((top_one.shape[0] + count * depth, blk_width), jnp.bfloat16),
    )(part.reshape(1), top_one, top_two)


def code_order(feats, dim, width):
    order = [0, *range(NPERM + 1, feats + 1), *range(1, NPERM + 1)]
    fixed = feats + 1 - NPERM

    def column(i, j):
        a, b = max(order[i], order[j]), min(order[i], order[j])
        return dim + a * (a - 1) // 2 + b

    cols = list(range(dim))
    cols += [column(i, j) for i in range(1, fixed) for j in range(i)]
    cols += [width - 1]
    cols += [-1] * (-len(cols) % 128)
    fixed_width = len(cols)
    cols += [column(i, j) for i in range(fixed, feats + 1) for j in range(i)]
    cols += [-1] * (-len(cols) % 128)
    return np.array(cols, np.int32), fixed_width


def fixed_codes(vectors, lead, fixed_width):
    gram = jnp.einsum("ird,jrd->rij", vectors, vectors, preferred_element_type=jnp.float32)
    pairs = [gram[:, level, :level] for level in range(1, vectors.shape[0])]
    out = jnp.concatenate([lead.astype(jnp.float32), *pairs], axis=1)
    return jnp.pad(out, ((0, 0), (0, fixed_width - out.shape[1]))).astype(jnp.bfloat16)


def moved_codes(moved, fixed, moved_width):
    every = jnp.concatenate([fixed, moved], axis=0)
    gram = jnp.einsum("ird,jrd->rij", moved, every, preferred_element_type=jnp.float32)
    pairs = [gram[:, i, : fixed.shape[0] + i] for i in range(moved.shape[0])]
    out = jnp.concatenate(pairs, axis=1)
    return jnp.pad(out, ((0, 0), (0, moved_width - out.shape[1]))).astype(jnp.bfloat16)


def top_kernel(codes_ref, cols_ref, weights_ref, out_w_ref, out_ref, acc_ref, codes_all_ref):
    step = pl.program_id(0)
    blk_width = weights_ref.shape[2]
    in_width = cols_ref.shape[1]
    in_rows = codes_all_ref.shape[1]
    fixed_width = 2 * in_width - codes_ref.shape[2]

    @pl.when(step == 0)
    def _():
        codes = jnp.concatenate([codes_ref[x] for x in range(codes_ref.shape[0])], axis=0)
        moved = jnp.concatenate([codes[:, :fixed_width], codes[:, in_width:]], axis=1)
        codes = jnp.concatenate([codes[:, :in_width], moved], axis=0)
        row = lax.broadcasted_iota(jnp.int32, (in_rows, in_width), 0)
        pick = jnp.where(row == cols_ref[...], 1.0, 0.0).astype(jnp.bfloat16)
        codes_all_ref[...] = lax.dot_general(
            codes, pick, (((1,), (1,)), ((), ())), preferred_element_type=jnp.float32
        ).astype(jnp.bfloat16)
        acc_ref[...] = jnp.zeros_like(acc_ref)

    codes = codes_all_ref[...]
    hidden = []
    for blk in range(weights_ref.shape[0]):
        pre = jnp.dot(codes, weights_ref[blk, :in_rows], preferred_element_type=jnp.float32)
        hidden.append(jnp.maximum(pre, 0.0).astype(jnp.bfloat16))
    for col in range(0, acc_ref.shape[1], blk_width):
        total = acc_ref[:, col : col + blk_width]
        row = in_rows + col
        for blk in range(weights_ref.shape[0]):
            total += jnp.dot(
                hidden[blk],
                weights_ref[blk, row : row + blk_width],
                preferred_element_type=jnp.float32,
            )
        acc_ref[:, col : col + blk_width] = total

    @pl.when(step == pl.num_programs(0) - 1)
    def _():
        xs, variants, row_count = out_ref.shape
        scaled = jnp.maximum(acc_ref[...], 0.0) * out_w_ref[...]
        folded = scaled[:, :128]
        for lane in range(128, scaled.shape[1], 128):
            folded += scaled[:, lane : lane + 128]
        sums = jnp.sum(folded.T, axis=0, keepdims=True)
        for variant in range(variants):
            for x in range(xs):
                start = (variant * xs + x) * row_count
                out_ref[x, variant : variant + 1] = sums[:, start : start + row_count]


def top_layers(codes, cols, weights, out_w):
    xs, row_count, _ = codes.shape
    groups, depth, blk_width = weights.shape
    steps = 2
    rows = 2 * xs * row_count
    return pl.pallas_call(
        top_kernel,
        grid=(steps,),
        in_specs=[
            pl.BlockSpec(memory_space=pltpu.VMEM),
            pl.BlockSpec(memory_space=pltpu.VMEM),
            pl.BlockSpec((groups // steps, depth, blk_width), lambda i: (i, 0, 0)),
            pl.BlockSpec(memory_space=pltpu.VMEM),
        ],
        out_specs=pl.BlockSpec((xs, 2, row_count), lambda i: (0, 0, 0)),
        scratch_shapes=[
            pltpu.VMEM((rows, out_w.shape[1]), jnp.float32),
            pltpu.VMEM((rows, depth - out_w.shape[1]), jnp.bfloat16),
        ],
        out_shape=jax.ShapeDtypeStruct((xs, 2, row_count), jnp.float32),
    )(codes, jnp.asarray(cols)[None], weights, out_w)


def local(
    dense_feats,
    sparse_ids,
    lengths,
    table_map,
    row_perm,
    tables,
    bottom_one,
    bottom_two,
    bottom_three,
    top_one,
    top_two,
    top_out,
):
    owners = lax.axis_size("tbl")
    owner_idx = lax.axis_index("tbl")
    xs = XS
    zs = owners // xs
    x_idx = owner_idx // zs
    along_x = [[x * zs + z for x in range(xs)] for z in range(zs)]
    out_cols = top_two.shape[1] // xs
    slot_count = tables.shape[0]
    row_count = dense_feats.shape[0]
    feats = sparse_ids.shape[0]
    dim = tables.shape[2]

    cols, fixed_width = code_order(feats, dim, top_one.shape[0])
    in_width = cols.shape[0]
    moved_width = in_width - fixed_width
    packed = pack_weights(x_idx.astype(jnp.int32), top_one, top_two, out_cols)
    weights = lax.all_gather(packed, "grp", axis=0, tiled=False)

    first_slot = (owner_idx * slot_count).astype(jnp.int32).reshape(1)
    pooled = pool_slots(
        table_map, first_slot, sparse_ids.transpose(0, 2, 1), lengths, tables, owners, row_count
    )
    arrived = lax.all_to_all(pooled, "tbl", split_axis=0, concat_axis=0, tiled=True)
    arrived = arrived.reshape(owners * slot_count, row_count, dim)
    pick_slot = (
        table_map[:, None] == jnp.arange(owners * slot_count, dtype=jnp.int32)[None, :]
    ).astype(jnp.bfloat16)
    embedded = jnp.einsum(
        "fs,srd->frd", pick_slot, arrived, preferred_element_type=jnp.float32
    ).astype(jnp.bfloat16)

    bottom_out = dense_layer(
        dense_layer(dense_layer(dense_feats, bottom_one), bottom_two), bottom_three
    )
    gathered = lax.all_gather(embedded[:NPERM], "grp", axis=1, tiled=True)
    fixed = jnp.concatenate([bottom_out[None], embedded[NPERM:]], axis=0)
    code_fixed = fixed_codes(fixed, bottom_out, fixed_width)
    code_base = moved_codes(embedded[:NPERM], fixed, moved_width)
    source = row_perm // (owners * row_count) * row_count + row_perm % row_count
    pick_row = (source[:, None] == jnp.arange(gathered.shape[1], dtype=jnp.int32)[None, :]).astype(
        jnp.bfloat16
    )
    shuffled = jnp.einsum(
        "rs,psd->prd", pick_row, gathered, preferred_element_type=jnp.float32
    ).astype(jnp.bfloat16)
    code_perm = moved_codes(shuffled, fixed, moved_width)
    codes = jnp.concatenate([code_fixed, code_base, code_perm], axis=1)
    codes_all = lax.all_to_all(
        jnp.broadcast_to(codes[None], (xs, *codes.shape)),
        "tbl",
        split_axis=0,
        concat_axis=0,
        tiled=True,
        axis_index_groups=along_x,
    )
    out_w = lax.dynamic_slice(top_out, (x_idx * out_cols,), (out_cols,)).reshape(1, out_cols)
    codes_all = pltpu.with_memory_space_constraint(codes_all, pltpu.VMEM)
    part = top_layers(codes_all, cols, weights, out_w.astype(jnp.float32))
    pieces = lax.all_to_all(
        part, "tbl", split_axis=0, concat_axis=0, tiled=True, axis_index_groups=along_x
    )
    return jax.nn.sigmoid(jnp.sum(pieces, axis=0))


def solution(mesh):
    placed = (
        P(("grp", "tbl"), None),
        P(None, "grp", None),
        P(None, "grp"),
        P(),
        P(("grp", "tbl")),
        P("tbl", None, None),
        P(),
        P(),
        P(),
        P(None, "grp"),
        P("grp", None),
        P(),
    )
    return jax.shard_map(
        local, mesh=mesh, in_specs=placed, out_specs=P(None, ("grp", "tbl")), check_vma=False
    )
```
